256 devices in a mesh: gx: 64 (over y_hi, z, x), gy: 4 (over y_lo, core).
Axes of the slice: x: 4, y: 4 (y_hi: 2, y_lo: 2; y = y_hi * 2 + y_lo), z: 8, core: 2. Of those that a mesh axis runs over, the one named last changes fastest.
Arguments:
- features: bfloat16 [2048, 512, 128], P(('gx', 'gy')), may hold values from -6 to 6
- weights: bfloat16 [27, 128, 128], replicated, may hold values from -0.109375 to 0.109375
- cotangent: bfloat16 [2048, 512, 128], P(('gx', 'gy')), may hold values from -6 to 6
- occupancy: int32 [2048, 512], P(('gx', 'gy')), may hold values 0 or 1
- slot_pos: int32 [2048], P(('gx', 'gy')), may hold values from -1 to 15, as said below
Outputs:
- outputs: bfloat16 [2048, 512, 128], P(('gx', 'gy'))
- grad_input: bfloat16 [2048, 512, 128], P(('gx', 'gy'))
- grad_weight: float32 [27, 128, 128], replicated
The draws below stay inside these ranges and needn't reach their ends.
Inputs may be any that keep to these rules, and one draw needn't show every extreme that they name: `slot_pos`: on each device the 8 slots name distinct positions of its region; live slots come first and the rest hold -1; each device has at least 4 live slots, and some device has all 8 live.
All inputs are finite; a program needn't handle non-finite values. No bound on the sum of `occupancy` on one device may be relied on, other than what follows from the above.
Results may differ from the reference program's by a relative error of at most 0.001.
Values may be sent and summed in bfloat16 or wider, within the bound.
No kernel may reach another device: no remote copies, remote signals or barrier semaphores. Data moves between devices by JAX's collectives and lax.ppermute only.
A program may use at most 64 MiB of HBM per device.

```python
import math
import jax
import jax.numpy as jnp
from jax import lax

CHANNELS = 128
BRICK = 8
REGION_X = 4
REGION_Y = 2
REGION_Z = 2
SLOTS = 8
BRICK_VOX = 512
ALL_SLOTS = 2048
N_GX = 64
N_GY = 4


def draw_slot_pos(key, part):
    devices = N_GX * N_GY
    positions = REGION_X * REGION_Y * REGION_Z
    count_key = jax.random.fold_in(key, 11)
    full_key = jax.random.fold_in(key, 23)
    order_key = jax.random.fold_in(key, 37)
    counts = jax.random.randint(count_key, (devices,), max(1, SLOTS // 2), SLOTS + 1)
    full_device = jax.random.randint(full_key, (), 0, devices)
    counts = jnp.where(jnp.arange(devices) == full_device, SLOTS, counts)

    def order_one(row_key):
        return jax.random.permutation(row_key, positions)
    orders = jax.vmap(order_one)(jax.random.split(order_key, devices))[:, :SLOTS]
    chosen = jnp.where(jnp.arange(SLOTS)[None, :] < counts[:, None], orders, -1)
    return chosen.reshape(devices * SLOTS).astype(jnp.int32)


def plant(entries, rng, low, top_value):
    dims = entries.shape
    index_at = [jax.random.randint(jax.random.fold_in(rng, axis), (), 0, dims[axis]) for axis in range(len(dims))]
    entries = entries.at[tuple(index_at)].set(low)
    longest = dims.index(max(dims))
    index_at[longest] = (index_at[longest] + 1) % dims[longest]
    return entries.at[tuple(index_at)].set(top_value)


def shard_levels(stream_key, dims, cuts, smallest, largest):
    factor_of, own = 1.0, jax.random.fold_in(stream_key, 6)
    for axis_at, parts in cuts:
        draws = jnp.exp(jax.random.uniform(jax.random.fold_in(own, axis_at), (parts,), jnp.float32, smallest / len(cuts), largest / len(cuts)))
        factor_of = factor_of * jnp.repeat(draws, dims[axis_at] // parts).reshape([-1 if axis == axis_at else 1 for axis in range(len(dims))])
    return factor_of


def scatter_about(key, extent, width, bound, shards=(), held_as=jnp.bfloat16):
    values = width * jax.random.normal(key, extent, jnp.float32)
    if shards:
        values = values * shard_levels(key, extent, shards, -0.22, 0.18)
    return jnp.clip(values, -bound, bound).astype(held_as)


def setup_inputs(seed: int = 0) -> dict:
    key_of = jax.random.split(jax.random.key(seed), 6)
    return {
        "features": scatter_about(key_of[0], (ALL_SLOTS, BRICK_VOX, CHANNELS), 1.0, 6.0, ((0, 256),)),
        "weights": scatter_about(key_of[1], (27, CHANNELS, CHANNELS), (27 * CHANNELS) ** -0.5, 0.109375),
        "cotangent": scatter_about(key_of[2], (ALL_SLOTS, BRICK_VOX, CHANNELS), 1.0, 6.0, ((0, 256),)),
        "occupancy": plant((jax.random.randint(key_of[3], (ALL_SLOTS, BRICK_VOX), 0, 16) < 15).astype(jnp.int32), jax.random.fold_in(key_of[3], 1), 0, 1),
        "slot_pos": draw_slot_pos(jax.random.fold_in(key_of[5], 71), 0),
    }


def offset_list():
    result = []
    for along_x in (-1, 0, 1):
        for along_y in (-1, 0, 1):
            for along_z in (-1, 0, 1):
                result.append((along_x, along_y, along_z))
    return result

def gather_patches(padded, corner, first_offset, offset_count):
    channels = padded.shape[-1]
    block_span = BRICK + 2
    starts = (corner[0], corner[1], corner[2], jnp.zeros((), jnp.int32))
    brick_block = lax.dynamic_slice(padded, starts, (block_span, block_span, block_span, channels))
    columns = []
    for along_x, along_y, along_z in offset_list()[first_offset:first_offset + offset_count]:
        window_cells = brick_block[along_x + 1:along_x + 1 + BRICK, along_y + 1:along_y + 1 + BRICK, along_z + 1:along_z + 1 + BRICK]
        columns.append(window_cells.reshape(BRICK ** 3, channels))
    return jnp.concatenate(columns, axis=1)

def map_grid(values, slot_pos):
    devices = N_GX * N_GY
    positions = REGION_X * REGION_Y * REGION_Z
    channels = values.shape[-1]
    table = jnp.zeros((devices, positions + 1, BRICK ** 3, channels), values.dtype)
    owner = jnp.repeat(jnp.arange(devices, dtype=jnp.int32), SLOTS)
    target = jnp.where(slot_pos >= 0, slot_pos, positions).astype(jnp.int32)
    table = table.at[owner, target].set(values)
    cells = table[:, :positions].reshape(N_GX, N_GY, REGION_X, REGION_Y, REGION_Z, BRICK, BRICK, BRICK, channels)
    cells = cells.transpose(0, 2, 5, 1, 3, 6, 4, 7, 8)
    cells = cells.reshape(N_GX * REGION_X * BRICK, N_GY * REGION_Y * BRICK, REGION_Z * BRICK, channels)
    return jnp.pad(cells, ((1, 1), (1, 1), (1, 1), (0, 0)))

def reference(features, weights, cotangent, occupancy, slot_pos):
    channels = features.shape[-1]
    voxels = BRICK ** 3
    active = (occupancy == 1) & (slot_pos >= 0)[:, None]
    zero_value = jnp.zeros((), features.dtype)
    masked_in = jnp.where(active[:, :, None], features, zero_value)
    masked_cot = jnp.where(active[:, :, None], cotangent, zero_value)
    grid_x = map_grid(masked_in, slot_pos)
    grid_dy = map_grid(masked_cot, slot_pos)
    w_forward = weights.astype(jnp.float32).reshape(27 * channels, channels)
    w_backward = weights[::-1].transpose(0, 2, 1).astype(jnp.float32).reshape(27 * channels, channels)
    highest = lax.Precision.HIGHEST

    def per_slot(slot_index, mask_row, cot_row):
        position = jnp.maximum(slot_pos[slot_index], 0).astype(jnp.int32)
        owner = (slot_index // SLOTS).astype(jnp.int32)
        gx_index = owner // N_GY
        gy_index = owner % N_GY
        corner = ((gx_index * REGION_X + position // (REGION_Y * REGION_Z)) * BRICK, (gy_index * REGION_Y + position // REGION_Z % REGION_Y) * BRICK, position % REGION_Z * BRICK)
        x_patches = gather_patches(grid_x, corner, 0, 27).astype(jnp.float32)
        dy_patches = gather_patches(grid_dy, corner, 0, 27).astype(jnp.float32)
        keep_mask = mask_row.astype(jnp.float32)[:, None]
        result = (jnp.dot(x_patches, w_forward, precision=highest) * keep_mask).astype(jnp.bfloat16)
        grad_in = (jnp.dot(dy_patches, w_backward, precision=highest) * keep_mask).astype(jnp.bfloat16)
        grad_w = jnp.dot(x_patches.T, cot_row.astype(jnp.float32), precision=highest)
        return (result, grad_in, grad_w)
    total_slots = slot_pos.shape[0]
    group_size = math.gcd(total_slots, 16)
    slot_ids = jnp.arange(total_slots, dtype=jnp.int32).reshape(-1, group_size)

    def per_group(pieces):
        results, grads, weight_terms = jax.vmap(per_slot)(pieces[0], pieces[1], pieces[2])
        return (results, grads, lax.optimization_barrier(jnp.sum(weight_terms, axis=0)))
    results, grads, weight_terms = lax.map(per_group, (slot_ids, active.reshape(-1, group_size, voxels), masked_cot.reshape(-1, group_size, voxels, channels)))
    scale = 1.0 / math.sqrt(float(total_slots * voxels))
    grad_weight = (lax.optimization_barrier(jnp.sum(weight_terms, axis=0)) * scale).reshape(27, channels, channels)
    outputs = results.reshape(total_slots, voxels, channels)
    grad_input = grads.reshape(total_slots, voxels, channels)
    return (outputs, grad_input, grad_weight)
```

```python
import itertools
import math

import jax
import jax.numpy as jnp
from jax import lax
from jax.experimental import pallas as pl
from jax.experimental.pallas import tpu as pltpu
from jax.sharding import Mesh, PartitionSpec as P

AXES = ("y_hi", "z", "x", "y_lo", "core")
SLOTS = 8
VOX = 512
CH = 128
NX, NY, NZ = 32, 16, 16
OFFSETS = 27
KROW = 9 * CH
BLOCKS = 16
BROWS = 112
F32 = jnp.float32
BF16 = jnp.bfloat16
VMEM = pl.BlockSpec(memory_space=pltpu.VMEM)
SMEM = pl.BlockSpec(memory_space=pltpu.SMEM)


def brick_of(pos):
    return pos >> 2, (pos >> 1) & 1, pos & 1


def mask_columns(occ_ref):
    return jnp.where(occ_ref[...] == 1, 1.0, 0.0).astype(F32).T


def place_kernel(pos_ref, occ_ref, feat_ref, cot_ref, xg_ref, cg_ref, lo_ref, hi_ref, yl_ref, yh_ref, xt_ref, cells):
    columns = mask_columns(occ_ref)
    for t, (src, dst) in enumerate(((cot_ref, cg_ref), (feat_ref, xg_ref))):

        def clear(x, carry):
            cells[x] = jnp.zeros((NY, 2, 8, CH), F32)
            return carry

        lax.fori_loop(0, NX, clear, 0)
        for s in range(SLOTS):
            pos = pos_ref[s]

            @pl.when(pos >= 0)
            def _():
                bx, by, bz = brick_of(pos)
                keep = jnp.broadcast_to(columns[:, s : s + 1], (VOX, CH))
                value = jnp.where(keep > 0.5, src[s].astype(F32), 0.0)
                cells[pl.ds(bx * 8, 8), pl.ds(by * 8, 8), bz] = value.reshape(8, 8, 8, CH)
                if t == 1:
                    xt_ref[s] = value.T.astype(BF16)

        def emit(x, carry):
            dst[x] = cells[x].reshape(NY, NZ, CH).astype(BF16)
            return carry

        lax.fori_loop(0, NX, emit, 0)
        lo_ref[t] = dst[0]
        hi_ref[t] = dst[NX - 1]
        yl_ref[t] = dst[:, 0]
        yh_ref[t] = dst[:, NY - 1]


def place(slot_pos, occupancy, features, cotangent):
    plane = jax.ShapeDtypeStruct((2, NY, NZ, CH), BF16)
    side = jax.ShapeDtypeStruct((2, NX, NZ, CH), BF16)
    grid = jax.ShapeDtypeStruct((NX, NY, NZ, CH), BF16)
    return pl.pallas_call(
        place_kernel,
        out_shape=(grid, grid, plane, plane, side, side, jax.ShapeDtypeStruct((SLOTS, CH, VOX), BF16)),
        in_specs=[SMEM, VMEM, VMEM, VMEM],
        out_specs=(VMEM,) * 7,
        scratch_shapes=[pltpu.VMEM((NX, NY, 2, 8, CH), F32)],
        compiler_params=pltpu.CompilerParams(vmem_limit_bytes=32 << 20),
        name="place",
    )(slot_pos, occupancy, features, cotangent)


def assemble(grid_ref, xlo_ref, xhi_ref, ylo_ref, yhi_ref, halo):
    def shifted(v):
        n = v.shape[0]
        flat = v.astype(F32).reshape(n * NZ, CH)
        z = lax.broadcasted_iota(jnp.int32, flat.shape, 0) & (NZ - 1)
        back = jnp.where(z == 0, 0.0, pltpu.roll(flat, 1, axis=0))
        ahead = jnp.where(z == NZ - 1, 0.0, pltpu.roll(flat, n * NZ - 1, axis=0))
        return [a.reshape(n, 2, 8, CH) for a in (back, flat, ahead)]

    def put_plane(x, v):
        for r, a in enumerate(shifted(v)):
            for bz in range(2):
                halo[r, bz, x, pl.ds(1, NY)] = a[:, bz]

    def body(x, carry):
        put_plane(x + 1, grid_ref[x])
        return carry

    lax.fori_loop(0, NX, body, 0)
    put_plane(0, xlo_ref[...])
    put_plane(NX + 1, xhi_ref[...])
    for y, ref in ((0, ylo_ref), (NY + 1, yhi_ref)):
        for r, a in enumerate(shifted(ref[...])):
            for bz in range(2):
                halo[r, bz, :, y] = a[:, bz]


def build_patches(pos, halo, patch_ref):
    bx, by, bz = brick_of(pos)
    for x in range(10):
        for q in range(3):
            for r in range(3):
                rows = halo[r, bz, bx * 8 + x, pl.ds(by * 8 + q, 8)]
                k = (q * 3 + r) * CH
                patch_ref[0, x, :, k : k + CH] = rows.reshape(64, CH).astype(BF16)


def patch_rows(patch_ref, p):
    return patch_ref[0, pl.ds(p, 8)].reshape(VOX, KROW)


def patches_kernel(pos_ref, grid_ref, xlo_ref, xhi_ref, ylo_ref, yhi_ref, patch_ref, halo):
    s = pl.program_id(0)

    @pl.when(s == 0)
    def _():
        assemble(grid_ref, xlo_ref, xhi_ref, ylo_ref, yhi_ref, halo)

    pos = pos_ref[s]

    @pl.when(pos >= 0)
    def _():
        build_patches(pos, halo, patch_ref)


def weight_kernel(pos_ref, meta_ref, grid_ref, xlo_ref, xhi_ref, ylo_ref, yhi_ref, xt_ref, patch_ref, keep_ref, send_ref, halo, total):
    s = pl.program_id(0)

    @pl.when(s == 0)
    def _():
        assemble(grid_ref, xlo_ref, xhi_ref, ylo_ref, yhi_ref, halo)

        def clear(o, carry):
            total[pl.ds(pl.multiple_of(o * CH, CH), CH)] = jnp.zeros((CH, CH), F32)
            return carry

        lax.fori_loop(0, OFFSETS + 1, clear, 0)

    pos = pos_ref[s]

    @pl.when(pos >= 0)
    def _():
        build_patches(pos, halo, patch_ref)
        for p in range(3):
            terms = jnp.dot(xt_ref[0], patch_rows(patch_ref, p), preferred_element_type=F32)
            for k in range(9):
                row = (OFFSETS - 1 - (p * 9 + k)) * CH
                total[row : row + CH] += terms[:, k * CH : (k + 1) * CH]

    @pl.when(s == SLOTS - 1)
    def _():
        core, own, other = meta_ref[0], meta_ref[1], meta_ref[2]

        def emit(j, carry):
            at = pl.multiple_of((core * BLOCKS + (j ^ own)) * BROWS, 8)
            keep_ref[j] = total[pl.ds(at, BROWS)]
            at = pl.multiple_of(((1 - core) * BLOCKS + (j ^ other)) * BROWS, 8)
            send_ref[j] = total[pl.ds(at, BROWS)]
            return carry

        lax.fori_loop(0, BLOCKS, emit, 0)


PATCH_SHAPE = jax.ShapeDtypeStruct((SLOTS, 10, 64, KROW), BF16)
PATCH_SPEC = pl.BlockSpec((1, 10, 64, KROW), lambda s, *_: (s, 0, 0, 0))
HALO = pltpu.VMEM((3, 2, NX + 2, NY + 2, 8, CH), F32)


def patches(slot_pos, grid, faces):
    return pl.pallas_call(
        patches_kernel,
        out_shape=PATCH_SHAPE,
        grid=(SLOTS,),
        in_specs=[SMEM] + [VMEM] * 5,
        out_specs=PATCH_SPEC,
        scratch_shapes=[HALO],
        compiler_params=pltpu.CompilerParams(vmem_limit_bytes=40 << 20),
        cost_estimate=pl.CostEstimate(flops=0, bytes_accessed=30 << 20, transcendentals=0),
        name="patches",
    )(slot_pos, grid, *faces)


def weight_gradient(slot_pos, meta, grid, faces, xt):
    half = jax.ShapeDtypeStruct((BLOCKS, BROWS, CH), F32)
    return pl.pallas_call(
        weight_kernel,
        out_shape=(PATCH_SHAPE, half, half),
        grid=(SLOTS,),
        in_specs=[SMEM, SMEM] + [VMEM] * 5 + [pl.BlockSpec((1, CH, VOX), lambda s: (s, 0, 0))],
        out_specs=(PATCH_SPEC, VMEM, VMEM),
        scratch_shapes=[HALO, pltpu.VMEM(((OFFSETS + 1) * CH, CH), F32)],
        compiler_params=pltpu.CompilerParams(vmem_limit_bytes=48 << 20),
        cost_estimate=pl.CostEstimate(flops=2 * 4096 * OFFSETS * CH * CH, bytes_accessed=30 << 20, transcendentals=0),
        name="weight_gradient",
    )(slot_pos, meta, grid, *faces, xt)


def conv_kernel(first, pos_ref, occ_ref, patch_ref, w_ref, *rest):
    out_ref = rest[-1]
    s = first + pl.program_id(0)
    pos = pos_ref[s]

    @pl.when(pos >= 0)
    def _():
        columns = mask_columns(occ_ref)
        total = jnp.dot(patch_rows(patch_ref, 0), w_ref[:KROW], preferred_element_type=F32)
        for p in range(1, 3):
            total += jnp.dot(patch_rows(patch_ref, p), w_ref[p * KROW : (p + 1) * KROW], preferred_element_type=F32)
        lane = lax.broadcasted_iota(jnp.int32, columns.shape, 1)
        keep = jnp.sum(jnp.where(lane == s, columns, 0.0), axis=1, keepdims=True)
        out_ref[0] = jnp.where(jnp.broadcast_to(keep, (VOX, CH)) > 0.5, total, 0.0).astype(BF16)

    @pl.when(pos < 0)
    def _():
        out_ref[0] = jnp.zeros((VOX, CH), BF16)


def convolve(slot_pos, occupancy, patch, weights, out, first, count):
    aliased = {} if out is None else {4: 0}
    extra = () if out is None else (out,)
    return pl.pallas_call(
        lambda *refs: conv_kernel(first, *refs),
        out_shape=jax.ShapeDtypeStruct((SLOTS, VOX, CH), BF16),
        grid=(count,),
        in_specs=[SMEM, VMEM, pl.BlockSpec((1, 10, 64, KROW), lambda i: (first + i, 0, 0, 0)), VMEM]
        + [pl.BlockSpec(memory_space=pl.ANY)] * len(extra),
        out_specs=pl.BlockSpec((1, VOX, CH), lambda i: (first + i, 0, 0)),
        input_output_aliases=aliased,
        compiler_params=pltpu.CompilerParams(vmem_limit_bytes=16 << 20),
        cost_estimate=pl.CostEstimate(flops=count * 4 * VOX * OFFSETS * CH * CH, bytes_accessed=count << 20, transcendentals=0),
        name="convolve",
    )(slot_pos, occupancy, patch, weights, *extra)


def finish_kernel(meta_ref, own_ref, other_ref, out_ref, rows):
    core, own, other = meta_ref[0], meta_ref[1], meta_ref[2]

    def place_block(j, carry):
        at = pl.multiple_of((core * BLOCKS + (j ^ own)) * BROWS, 8)
        rows[pl.ds(at, BROWS)] = own_ref[j]
        at = pl.multiple_of(((1 - core) * BLOCKS + (j ^ other)) * BROWS, 8)
        rows[pl.ds(at, BROWS)] = other_ref[j]
        return carry

    lax.fori_loop(0, BLOCKS, place_block, 0)
    scale = 1.0 / math.sqrt(float(256 * SLOTS * VOX))

    def emit(o, carry):
        out_ref[o] = rows[pl.ds(pl.multiple_of(o * CH, CH), CH)] * scale
        return carry

    lax.fori_loop(0, OFFSETS, emit, 0)


def finish(meta, own, other):
    return pl.pallas_call(
        finish_kernel,
        out_shape=jax.ShapeDtypeStruct((OFFSETS, CH, CH), F32),
        in_specs=[SMEM, VMEM, VMEM],
        out_specs=VMEM,
        scratch_shapes=[pltpu.VMEM(((OFFSETS + 1) * CH, CH), F32)],
        compiler_params=pltpu.CompilerParams(vmem_limit_bytes=24 << 20),
        name="finish",
    )(meta, own, other)


def make_shards(sizes):
    everyone = list(itertools.product(*[range(n) for n in sizes]))
    n_y_lo, n_core = sizes[3], sizes[4]
    narrow = n_y_lo * n_core
    wide = len(everyone) // narrow

    def number(at):
        flat = 0
        for a, n in zip(at, sizes):
            flat = flat * n + a
        return flat

    def mate(at, axis, k):
        y_hi, z, x, y_lo, core = at
        if isinstance(axis, tuple):
            axis = axis[core]
        y = y_hi * n_y_lo + y_lo
        if axis == "core":
            core ^= k
        elif axis == "x":
            x ^= k
        elif axis == "y":
            y ^= k
        else:
            z ^= k
        return (y // n_y_lo, z, x, y % n_y_lo, core)

    def swap(value, axis, k):
        return lax.ppermute(value, AXES, [(number(a), number(mate(a, axis, k))) for a in everyone])

    def shift_wide(value, step):
        pairs = [(i * narrow + j, (i + step) * narrow + j) for i in range(wide) for j in range(narrow) if 0 <= i + step < wide]
        return lax.ppermute(value, AXES, pairs)

    def shift_narrow(value, step):
        pairs = [(i * narrow + j, i * narrow + j + step) for i in range(wide) for j in range(narrow) if 0 <= j + step < narrow]
        return lax.ppermute(value, AXES, pairs)

    first, second = ("y", "x"), ("x", "y")

    def scatter(value, axis):
        n = value.shape[0] // 4
        parts = [swap(value[k * n : (k + 1) * n], axis, k) for k in (2, 1, 3)]
        return value[:n] + parts[0] + parts[1] + parts[2]

    def gather(value, axis):
        got = {k: swap(value, axis, k) for k in (2, 1, 3)}
        return jnp.concatenate([value, got[1], got[2], got[3]], axis=0)

    def double(value, axis, ks):
        total = value
        for part in [swap(value, axis, k) for k in ks]:
            total = total + part
        return total

    def shards(features, weights, cotangent, occupancy, slot_pos):
        core = lax.axis_index("core")
        x_at = lax.axis_index("x")
        y_at = lax.axis_index("y_hi") * n_y_lo + lax.axis_index("y_lo")
        yx, xy = y_at * 4 + x_at, x_at * 4 + y_at
        meta = jnp.stack([core, jnp.where(core == 0, yx, xy), jnp.where(core == 0, xy, yx)]).astype(jnp.int32)
        xg, cg, lo, hi, side_lo, side_hi, xt = place(slot_pos, occupancy, features, cotangent)
        before = shift_wide(hi, 1)
        after = shift_wide(lo, -1)
        rim_hi = jnp.concatenate([before[:, None, NY - 1], side_hi, after[:, None, NY - 1]], axis=1)
        rim_lo = jnp.concatenate([before[:, None, 0], side_lo, after[:, None, 0]], axis=1)
        left = shift_narrow(rim_hi, 1)
        right = shift_narrow(rim_lo, -1)
        cot_faces = (before[0], after[0], left[0], right[0])
        in_faces = (before[1], after[1], left[1], right[1])
        cot_patch, keep, send = weight_gradient(slot_pos, meta, cg, cot_faces, xt)
        in_patch = patches(slot_pos, xg, in_faces)
        w_forward = weights.reshape(OFFSETS * CH, CH)
        w_backward = weights[::-1].transpose(0, 2, 1).reshape(OFFSETS * CH, CH)

        total = keep + swap(send, "core", 1)
        total = scatter(total, first)
        total = scatter(total, second)
        total = double(total, "z", (2, 1, 3))
        total = double(total, "z", (4,))
        total = gather(total, second)
        total = gather(total, first)
        grad_weight = finish(meta, total, swap(total, "core", 1))

        outputs = grad_input = None
        for s in range(0, SLOTS, 2):
            outputs = convolve(slot_pos, occupancy, in_patch, w_forward, outputs, s, 2)
        for s in range(0, SLOTS, 2):
            grad_input = convolve(slot_pos, occupancy, cot_patch, w_backward, grad_input, s, 2)
        return outputs, grad_input, grad_weight

    return shards


def solution(mesh):
    sizes = (2, 8, 4, 2, 2)
    fine = Mesh(mesh.devices.reshape(sizes), AXES)
    return jax.shard_map(
        make_shards(sizes),
        mesh=fine,
        in_specs=(P(AXES, None, None), P(), P(AXES, None, None), P(AXES, None), P(AXES)),
        out_specs=(P(AXES, None, None), P(AXES, None, None), P()),
        check_vma=False,
    )
```

```python
import itertools
import math

import jax
import jax.numpy as jnp
from jax import lax
from jax.experimental import pallas as pl
from jax.experimental.pallas import tpu as pltpu
from jax.sharding import Mesh, PartitionSpec as P

AXES = ("y_hi", "z", "x", "y_lo", "core")
SLOTS = 8
VOX = 512
CH = 128
NX, NY, NZ = 32, 16, 16
OFFSETS = 27
KROW = 9 * CH
BLOCKS = 16
BROWS = 112
F32 = jnp.float32
BF16 = jnp.bfloat16
VMEM = pl.BlockSpec(memory_space=pltpu.VMEM)
SMEM = pl.BlockSpec(memory_space=pltpu.SMEM)


def pin(value, space):
    return pltpu.with_memory_space_constraint(value, space)


def brick_of(pos):
    return pos >> 2, (pos >> 1) & 1, pos & 1


def mask_columns(occ_ref):
    return jnp.where(occ_ref[...] == 1, 1.0, 0.0).astype(F32).T


def place_kernel(pos_ref, meta_ref, occ_ref, feat_hbm, cot_hbm, xg_hbm, cg_hbm, xt_hbm, even_ref, odd_ref, side_even_ref, side_odd_ref, cells, slots, grids, xt, load_sems, grid_sems, xt_sem):
    def load(t, s):
        return pltpu.make_async_copy((cot_hbm, feat_hbm)[t].at[s], slots.at[t, s], load_sems.at[t, s])

    def save(t, n):
        part = pl.ds(n * 8, 8)
        return pltpu.make_async_copy(grids.at[t, part], (cg_hbm, xg_hbm)[t].at[part], grid_sems.at[t, n])

    for t in range(2):
        for s in range(SLOTS):
            load(t, s).start()
    columns = mask_columns(occ_ref)
    core, odd_x = meta_ref[0], meta_ref[3]
    for t in range(2):

        def clear(x, carry):
            cells[x] = jnp.zeros((NY, 2, 8, CH), F32)
            return carry

        lax.fori_loop(0, NX, clear, 0)
        for s in range(SLOTS):
            load(t, s).wait()
            pos = pos_ref[s]

            @pl.when(pos >= 0)
            def _():
                bx, by, bz = brick_of(pos)
                keep = jnp.broadcast_to(columns[:, s : s + 1], (VOX, CH))
                value = jnp.where(keep > 0.5, slots[t, s].astype(F32), 0.0)
                cells[pl.ds(bx * 8, 8), pl.ds(by * 8, 8), bz] = value.reshape(8, 8, 8, CH)
                if t == 1:
                    xt[s] = value.T.astype(BF16)

        if t == 1:
            save_xt = pltpu.make_async_copy(xt, xt_hbm, xt_sem)
            save_xt.start()

        def emit(x, carry):
            grids[t, x] = cells[x].reshape(NY, NZ, CH).astype(BF16)
            return carry

        for n in range(4):
            lax.fori_loop(n * 8, n * 8 + 8, emit, 0)
            save(t, n).start()
        even_ref[t] = grids[t, (NX - 1) * (1 - odd_x)]
        odd_ref[t] = grids[t, (NX - 1) * odd_x]
        side_even_ref[t] = grids[t, :, (NY - 1) * (1 - core)]
        side_odd_ref[t] = grids[t, :, (NY - 1) * core]
    save_xt.wait()
    for t in range(2):
        for n in range(4):
            save(t, n).wait()


def place(slot_pos, meta, occupancy, features, cotangent):
    plane = jax.ShapeDtypeStruct((2, NY, NZ, CH), BF16)
    side = jax.ShapeDtypeStruct((2, NX, NZ, CH), BF16)
    grid = pltpu.HBM((NX, NY, NZ, CH), BF16)
    hbm = pl.BlockSpec(memory_space=pltpu.HBM)
    return pl.pallas_call(
        place_kernel,
        out_shape=(grid, grid, pltpu.HBM((SLOTS, CH, VOX), BF16), plane, plane, side, side),
        in_specs=[SMEM, SMEM, VMEM, hbm, hbm],
        out_specs=(hbm,) * 3 + (VMEM,) * 4,
        scratch_shapes=[
            pltpu.VMEM((NX, NY, 2, 8, CH), F32),
            pltpu.VMEM((2, SLOTS, VOX, CH), BF16),
            pltpu.VMEM((2, NX, NY, NZ, CH), BF16),
            pltpu.VMEM((SLOTS, CH, VOX), BF16),
            pltpu.SemaphoreType.DMA((2, SLOTS)),
            pltpu.SemaphoreType.DMA((2, 4)),
            pltpu.SemaphoreType.DMA,
        ],
        compiler_params=pltpu.CompilerParams(vmem_limit_bytes=24 << 20),
        name="place",
    )(slot_pos, meta, occupancy, pin(features, pltpu.HBM), pin(cotangent, pltpu.HBM))


def assemble(meta_ref, grid_ref, even_ref, odd_ref, side_even_ref, side_odd_ref, halo):
    core, odd_x = meta_ref[0], meta_ref[3]

    def shifted(v):
        n = v.shape[0]
        flat = v.astype(F32).reshape(n * NZ, CH)
        z = lax.broadcasted_iota(jnp.int32, flat.shape, 0) & (NZ - 1)
        back = jnp.where(z == 0, 0.0, pltpu.roll(flat, 1, axis=0))
        ahead = jnp.where(z == NZ - 1, 0.0, pltpu.roll(flat, n * NZ - 1, axis=0))
        return [a.reshape(n, 2, 8, CH) for a in (back, flat, ahead)]

    def put_plane(x, v):
        for r, a in enumerate(shifted(v)):
            for bz in range(2):
                halo[r, bz, x, pl.ds(1, NY)] = a[:, bz]

    def body(x, carry):
        put_plane(x + 1, grid_ref[x])
        return carry

    lax.fori_loop(0, NX, body, 0)
    put_plane((NX + 1) * (1 - odd_x), even_ref[...])
    put_plane((NX + 1) * odd_x, odd_ref[...])
    for y, ref in (((NY + 1) * (1 - core), side_even_ref), ((NY + 1) * core, side_odd_ref)):
        for r, a in enumerate(shifted(ref[...])):
            for bz in range(2):
                halo[r, bz, :, y] = a[:, bz]


def build_patches(pos, halo, patch_ref):
    bx, by, bz = brick_of(pos)
    for x in range(10):
        for q in range(3):
            for r in range(3):
                rows = halo[r, bz, bx * 8 + x, pl.ds(by * 8 + q, 8)]
                k = (q * 3 + r) * CH
                patch_ref[0, x, :, k : k + CH] = rows.reshape(64, CH).astype(BF16)


def patch_rows(patch_ref, p):
    return patch_ref[0, pl.ds(p, 8)].reshape(VOX, KROW)


def patches_kernel(pos_ref, meta_ref, *refs):
    patch_ref, halo = refs[5:]
    s = pl.program_id(0)

    @pl.when(s == 0)
    def _():
        assemble(meta_ref, *refs[:5], halo)

    pos = pos_ref[s]

    @pl.when(pos >= 0)
    def _():
        build_patches(pos, halo, patch_ref)


def weight_kernel(pos_ref, meta_ref, *refs):
    xt_ref, patch_ref, keep_ref, send_ref, halo, total = refs[5:]
    s = pl.program_id(0)

    @pl.when(s == 0)
    def _():
        assemble(meta_ref, *refs[:5], halo)

        def clear(o, carry):
            total[pl.ds(pl.multiple_of(o * CH, CH), CH)] = jnp.zeros((CH, CH), F32)
            return carry

        lax.fori_loop(0, OFFSETS + 1, clear, 0)

    pos = pos_ref[s]

    @pl.when(pos >= 0)
    def _():
        build_patches(pos, halo, patch_ref)
        for p in range(3):
            terms = jnp.dot(xt_ref[0], patch_rows(patch_ref, p), preferred_element_type=F32)
            for k in range(9):
                row = (OFFSETS - 1 - (p * 9 + k)) * CH
                total[row : row + CH] += terms[:, k * CH : (k + 1) * CH]

    @pl.when(s == SLOTS - 1)
    def _():
        core, own, other = meta_ref[0], meta_ref[1], meta_ref[2]

        def emit(j, carry):
            at = pl.multiple_of((core * BLOCKS + (j ^ own)) * BROWS, 8)
            keep_ref[j] = total[pl.ds(at, BROWS)]
            at = pl.multiple_of(((1 - core) * BLOCKS + (j ^ other)) * BROWS, 8)
            send_ref[j] = total[pl.ds(at, BROWS)]
            return carry

        lax.fori_loop(0, BLOCKS, emit, 0)


PATCH_SHAPE = pltpu.HBM((SLOTS, 10, 64, KROW), BF16)
PATCH_SPEC = pl.BlockSpec((1, 10, 64, KROW), lambda s, *_: (s, 0, 0, 0))
HALO = pltpu.VMEM((3, 2, NX + 2, NY + 2, 8, CH), F32)


def patches(slot_pos, meta, grid, faces):
    return pl.pallas_call(
        patches_kernel,
        out_shape=PATCH_SHAPE,
        grid=(SLOTS,),
        in_specs=[SMEM, SMEM] + [VMEM] * 5,
        out_specs=PATCH_SPEC,
        scratch_shapes=[HALO],
        compiler_params=pltpu.CompilerParams(vmem_limit_bytes=28 << 20),
        cost_estimate=pl.CostEstimate(flops=0, bytes_accessed=30 << 20, transcendentals=0),
        name="patches",
    )(slot_pos, meta, grid, *faces)


def weight_gradient(slot_pos, meta, grid, faces, xt):
    half = pltpu.VMEM((BLOCKS, BROWS, CH), F32)
    return pl.pallas_call(
        weight_kernel,
        out_shape=(PATCH_SHAPE, half, half),
        grid=(SLOTS,),
        in_specs=[SMEM, SMEM] + [VMEM] * 5 + [pl.BlockSpec((1, CH, VOX), lambda s: (s, 0, 0))],
        out_specs=(PATCH_SPEC, VMEM, VMEM),
        scratch_shapes=[HALO, pltpu.VMEM(((OFFSETS + 1) * CH, CH), F32)],
        compiler_params=pltpu.CompilerParams(vmem_limit_bytes=32 << 20),
        cost_estimate=pl.CostEstimate(flops=2 * 4096 * OFFSETS * CH * CH, bytes_accessed=30 << 20, transcendentals=0),
        name="weight_gradient",
    )(slot_pos, meta, grid, *faces, xt)


def conv_kernel(first, pos_ref, occ_ref, patch_ref, w_ref, *rest):
    out_ref = rest[-1]
    s = first + pl.program_id(0)
    pos = pos_ref[s]

    @pl.when(pos >= 0)
    def _():
        columns = mask_columns(occ_ref)
        total = jnp.dot(patch_rows(patch_ref, 0), w_ref[:KROW], preferred_element_type=F32)
        for p in range(1, 3):
            total += jnp.dot(patch_rows(patch_ref, p), w_ref[p * KROW : (p + 1) * KROW], preferred_element_type=F32)
        lane = lax.broadcasted_iota(jnp.int32, columns.shape, 1)
        keep = jnp.sum(jnp.where(lane == s, columns, 0.0), axis=1, keepdims=True)
        out_ref[0] = jnp.where(jnp.broadcast_to(keep, (VOX, CH)) > 0.5, total, 0.0).astype(BF16)

    @pl.when(pos < 0)
    def _():
        out_ref[0] = jnp.zeros((VOX, CH), BF16)


def convolve(slot_pos, occupancy, patch, weights, out, first, count):
    aliased = {} if out is None else {4: 0}
    extra = () if out is None else (out,)
    return pl.pallas_call(
        lambda *refs: conv_kernel(first, *refs),
        out_shape=jax.ShapeDtypeStruct((SLOTS, VOX, CH), BF16),
        grid=(count,),
        in_specs=[SMEM, VMEM, pl.BlockSpec((1, 10, 64, KROW), lambda i: (first + i, 0, 0, 0)), VMEM]
        + [pl.BlockSpec(memory_space=pl.ANY)] * len(extra),
        out_specs=pl.BlockSpec((1, VOX, CH), lambda i: (first + i, 0, 0)),
        input_output_aliases=aliased,
        compiler_params=pltpu.CompilerParams(vmem_limit_bytes=16 << 20),
        cost_estimate=pl.CostEstimate(flops=count * 4 * VOX * OFFSETS * CH * CH, bytes_accessed=count << 20, transcendentals=0),
        name="convolve",
    )(slot_pos, occupancy, pin(patch, pltpu.HBM), weights, *extra)


def finish_kernel(meta_ref, own_ref, other_ref, out_ref, rows):
    core, own, other = meta_ref[0], meta_ref[1], meta_ref[2]

    def place_block(j, carry):
        at = pl.multiple_of((core * BLOCKS + (j ^ own)) * BROWS, 8)
        rows[pl.ds(at, BROWS)] = own_ref[j]
        at = pl.multiple_of(((1 - core) * BLOCKS + (j ^ other)) * BROWS, 8)
        rows[pl.ds(at, BROWS)] = other_ref[j]
        return carry

    lax.fori_loop(0, BLOCKS, place_block, 0)
    scale = 1.0 / math.sqrt(float(256 * SLOTS * VOX))

    def emit(o, carry):
        out_ref[o] = rows[pl.ds(pl.multiple_of(o * CH, CH), CH)] * scale
        return carry

    lax.fori_loop(0, OFFSETS, emit, 0)


def finish(meta, own, other):
    return pl.pallas_call(
        finish_kernel,
        out_shape=jax.ShapeDtypeStruct((OFFSETS, CH, CH), F32),
        in_specs=[SMEM, VMEM, VMEM],
        out_specs=VMEM,
        scratch_shapes=[pltpu.VMEM(((OFFSETS + 1) * CH, CH), F32)],
        compiler_params=pltpu.CompilerParams(vmem_limit_bytes=24 << 20),
        name="finish",
    )(meta, own, other)


def make_shards(sizes):
    everyone = list(itertools.product(*[range(n) for n in sizes]))
    n_y_lo, n_core = sizes[3], sizes[4]
    narrow = n_y_lo * n_core
    wide = len(everyone) // narrow

    def number(at):
        flat = 0
        for a, n in zip(at, sizes):
            flat = flat * n + a
        return flat

    def mate(at, axis, k):
        y_hi, z, x, y_lo, core = at
        if isinstance(axis, tuple):
            axis = axis[core]
        y = y_hi * n_y_lo + y_lo
        if axis == "core":
            core ^= k
        elif axis == "x":
            x ^= k
        elif axis == "y":
            y ^= k
        else:
            z ^= k
        return (y // n_y_lo, z, x, y % n_y_lo, core)

    def swap(value, axis, k):
        return lax.ppermute(value, AXES, [(number(a), number(mate(a, axis, k))) for a in everyone])

    def exchange_wide(value, start):
        pairs = [(i * narrow + j, k * narrow + j) for a in range(start, wide - 1, 2) for i, k in ((a, a + 1), (a + 1, a)) for j in range(narrow)]
        return lax.ppermute(value, AXES, pairs)

    def exchange_narrow(value, start):
        pairs = [(i * narrow + j, i * narrow + k) for i in range(wide) for a in range(start, narrow - 1, 2) for j, k in ((a, a + 1), (a + 1, a))]
        return lax.ppermute(value, AXES, pairs)

    first, second = ("y", "x"), ("x", "y")

    def tie(*values):
        return lax.optimization_barrier(values)

    def scatter(value, axis):
        n = value.shape[0] // 4
        return [swap(value[k * n : (k + 1) * n], axis, k) for k in (2, 1, 3)]

    def add(value, parts):
        total = value[: parts[0].shape[0]]
        for part in parts:
            total = total + part
        return total

    def copies(value, axis, ks):
        return [swap(value, axis, k) for k in ks]

    def join(value, parts):
        return jnp.concatenate([value, parts[1], parts[0], parts[2]], axis=0)

    def shards(features, weights, cotangent, occupancy, slot_pos):
        core = lax.axis_index("core")
        x_at = lax.axis_index("x")
        y_at = lax.axis_index("y_hi") * n_y_lo + lax.axis_index("y_lo")
        yx, xy = y_at * 4 + x_at, x_at * 4 + y_at
        odd_x = x_at & 1
        meta = jnp.stack([core, jnp.where(core == 0, yx, xy), jnp.where(core == 0, xy, yx), odd_x]).astype(jnp.int32)
        xg, cg, xt, even, odd, side_even, side_odd = place(slot_pos, meta, occupancy, features, cotangent)
        even, odd, source = tie(even, odd, weights)
        even = exchange_wide(even, 0)
        odd = exchange_wide(odd, 1)
        w_backward = source[::-1].transpose(0, 2, 1).reshape(OFFSETS * CH, CH)
        even, odd, w_backward = tie(even, odd, w_backward)
        before, after = jnp.where(odd_x == 0, odd, even), jnp.where(odd_x == 0, even, odd)

        def rim(side, top):
            ends = [jnp.where(top, v[:, None, NY - 1], v[:, None, 0]) for v in (before, after)]
            return jnp.concatenate([ends[0], side, ends[1]], axis=1)

        side_even = exchange_narrow(rim(side_even, core == 0), 0)
        side_odd = exchange_narrow(rim(side_odd, core == 1), 1)
        faces = (even, odd, side_even, side_odd)
        cot_patch, keep, send = weight_gradient(slot_pos, meta, cg, [f[0] for f in faces], xt)
        w_forward = weights.reshape(OFFSETS * CH, CH)
        done = {"outputs": None, "grad_input": None, "patch": None}

        def backward(at, pos):
            done["grad_input"] = convolve(pos, occupancy, cot_patch, w_backward, done["grad_input"], *at)
            return "grad_input"

        def forward(at, pos):
            done["outputs"] = convolve(pos, occupancy, done["patch"], w_forward, done["outputs"], *at)
            return "outputs"

        def gather_patches(at, pos):
            done["patch"] = patches(pos, meta, xg, [f[1] for f in faces])
            return "patch"

        def stage(value, start, *work):
            value, pos = tie(value, slot_pos)
            parts = start(value)
            names = {call(at, pos) for call, at in work}
            held = tie(parts, *[done[n] for n in sorted(names)])
            for n, v in zip(sorted(names), held[1:]):
                done[n] = v
            return value, held[0]

        _, (got,) = stage(send, lambda v: copies(v, "core", (1,)), (backward, (0, 1)))
        total = keep + got
        total = add(*stage(total, lambda v: scatter(v, first), (backward, (1, 4))))
        total = add(*stage(total, lambda v: scatter(v, second), (backward, (5, 2))))
        total = add(*stage(total, lambda v: copies(v, "z", (2, 1, 3)), (gather_patches, None)))
        total = add(*stage(total, lambda v: copies(v, "z", (4,)), (backward, (7, 1)), (forward, (0, 1))))
        total = join(*stage(total, lambda v: copies(v, second, (2, 1, 3)), (forward, (1, 2))))
        total = join(*stage(total, lambda v: copies(v, first, (2, 1, 3)), (forward, (3, 4))))
        total, (got,) = stage(total, lambda v: copies(v, "core", (1,)), (forward, (7, 1)))
        grad_weight = finish(meta, total, got)
        return done["outputs"], done["grad_input"], grad_weight

    return shards


def solution(mesh):
    sizes = (2, 8, 4, 2, 2)
    fine = Mesh(mesh.devices.reshape(sizes), AXES)
    return jax.shard_map(
        make_shards(sizes),
        mesh=fine,
        in_specs=(P(AXES, None, None), P(), P(AXES, None, None), P(AXES, None), P(AXES)),
        out_specs=(P(AXES, None, None), P(AXES, None, None), P()),
        check_vma=False,
    )
```

```python
import itertools
import math

import jax
import jax.numpy as jnp
from jax import lax
from jax.experimental import pallas as pl
from jax.experimental.pallas import tpu as pltpu
from jax.sharding import Mesh, PartitionSpec as P

AXES = ("y_hi", "z", "x", "y_lo", "core")
SLOTS = 8
VOX = 512
CH = 128
NX, NY, NZ = 32, 16, 16
OFFSETS = 27
KROW = 9 * CH
BLOCKS = 16
BROWS = 112
PROWS = 80
F32 = jnp.float32
BF16 = jnp.bfloat16
VMEM = pl.BlockSpec(memory_space=pltpu.VMEM)
SMEM = pl.BlockSpec(memory_space=pltpu.SMEM)


def pin(value, space):
    return pltpu.with_memory_space_constraint(value, space)


def brick_of(pos):
    return pos >> 2, (pos >> 1) & 1, pos & 1


def mask_columns(occ_ref):
    return jnp.where(occ_ref[...] == 1, 1.0, 0.0).astype(F32).T


def place_kernel(pos_ref, meta_ref, occ_ref, feat_hbm, cot_hbm, xg_hbm, cg_hbm, xt_hbm, even_ref, odd_ref, side_even_ref, side_odd_ref, cells, slots, grids, xt, load_sems, grid_sems, xt_sem):
    def load(t, s):
        return pltpu.make_async_copy((cot_hbm, feat_hbm)[t].at[s], slots.at[t, s], load_sems.at[t, s])

    def save(t, n):
        part = pl.ds(n * 8, 8)
        return pltpu.make_async_copy(grids.at[t, part], (cg_hbm, xg_hbm)[t].at[part], grid_sems.at[t, n])

    for t in range(2):
        for s in range(SLOTS):
            load(t, s).start()
    columns = mask_columns(occ_ref)
    core, odd_x = meta_ref[0], meta_ref[3]
    for t in range(2):

        def clear(x, carry):
            cells[x] = jnp.zeros((NY, 2, 8, CH), F32)
            return carry

        lax.fori_loop(0, NX, clear, 0)
        for s in range(SLOTS):
            load(t, s).wait()
            pos = pos_ref[s]

            @pl.when(pos >= 0)
            def _():
                bx, by, bz = brick_of(pos)
                keep = jnp.broadcast_to(columns[:, s : s + 1], (VOX, CH))
                value = jnp.where(keep > 0.5, slots[t, s].astype(F32), 0.0)
                cells[pl.ds(bx * 8, 8), pl.ds(by * 8, 8), bz] = value.reshape(8, 8, 8, CH)
                if t == 1:
                    xt[s] = value.T.astype(BF16)

        if t == 1:
            save_xt = pltpu.make_async_copy(xt, xt_hbm, xt_sem)
            save_xt.start()

        def emit(x, carry):
            grids[t, x] = cells[x].reshape(NY, NZ, CH).astype(BF16)
            return carry

        for n in range(4):
            lax.fori_loop(n * 8, n * 8 + 8, emit, 0)
            save(t, n).start()
        even_ref[t] = grids[t, (NX - 1) * (1 - odd_x)]
        odd_ref[t] = grids[t, (NX - 1) * odd_x]
        side_even_ref[t] = grids[t, :, (NY - 1) * (1 - core)]
        side_odd_ref[t] = grids[t, :, (NY - 1) * core]
    save_xt.wait()
    for t in range(2):
        for n in range(4):
            save(t, n).wait()


def place(slot_pos, meta, occupancy, features, cotangent):
    plane = jax.ShapeDtypeStruct((2, NY, NZ, CH), BF16)
    side = jax.ShapeDtypeStruct((2, NX, NZ, CH), BF16)
    grid = pltpu.HBM((NX, NY, NZ, CH), BF16)
    hbm = pl.BlockSpec(memory_space=pltpu.HBM)
    return pl.pallas_call(
        place_kernel,
        out_shape=(grid, grid, pltpu.HBM((SLOTS, CH, VOX), BF16), plane, plane, side, side),
        in_specs=[SMEM, SMEM, VMEM, hbm, hbm],
        out_specs=(hbm,) * 3 + (VMEM,) * 4,
        scratch_shapes=[
            pltpu.VMEM((NX, NY, 2, 8, CH), F32),
            pltpu.VMEM((2, SLOTS, VOX, CH), BF16),
            pltpu.VMEM((2, NX, NY, NZ, CH), BF16),
            pltpu.VMEM((SLOTS, CH, VOX), BF16),
            pltpu.SemaphoreType.DMA((2, SLOTS)),
            pltpu.SemaphoreType.DMA((2, 4)),
            pltpu.SemaphoreType.DMA,
        ],
        compiler_params=pltpu.CompilerParams(vmem_limit_bytes=24 << 20),
        name="place",
    )(slot_pos, meta, occupancy, pin(features, pltpu.HBM), pin(cotangent, pltpu.HBM))


def shifted(v):
    n = v.shape[0]
    flat = v.astype(F32).reshape(n * NZ, CH)
    z = lax.broadcasted_iota(jnp.int32, flat.shape, 0) & (NZ - 1)
    back = jnp.where(z == 0, 0.0, pltpu.roll(flat, 1, axis=0))
    ahead = jnp.where(z == NZ - 1, 0.0, pltpu.roll(flat, n * NZ - 1, axis=0))
    return [a.reshape(n, 2, 8, CH) for a in (back, flat, ahead)]


def assemble(meta_ref, grid_ref, side_even_ref, side_odd_ref, halo, planes=None):
    core, odd_x = meta_ref[0], meta_ref[3]

    def body(x, carry):
        for r, a in enumerate(shifted(grid_ref[x])):
            for bz in range(2):
                halo[r, bz, x + 1, pl.ds(1, NY)] = a[:, bz]
        return carry

    lax.fori_loop(0, NX, body, 0)
    for y, ref in (((NY + 1) * (1 - core), side_even_ref), ((NY + 1) * core, side_odd_ref)):
        for r, a in enumerate(shifted(ref[...])):
            for bz in range(2):
                halo[r, bz, pl.ds(1, NX), y] = a[:, bz]
    for i, x in enumerate(((NX + 1) * (1 - odd_x), (NX + 1) * odd_x)):
        if planes is None:
            halo[:, :, x] = jnp.zeros((3, 2, NY + 2, 8, CH), F32)
        else:
            for r, a in enumerate(shifted(planes[i][...])):
                for bz in range(2):
                    halo[r, bz, x] = a[:, bz]


def build_patches(pos, halo, patch_ref):
    bx, by, bz = brick_of(pos)
    for x in range(10):
        for r in range(3):
            rows = halo[r, bz, bx * 8 + x, pl.ds(by * 8, 10)]
            patch_ref[0, x, :, r * CH : (r + 1) * CH] = rows.reshape(PROWS, CH).astype(BF16)


def patch_rows(patch_ref, p):
    parts = [patch_ref[0, pl.ds(p, 8), pl.ds(q * 8, 64)].reshape(VOX, 3 * CH) for q in range(3)]
    return jnp.concatenate(parts, axis=1)


def patches_kernel(pos_ref, meta_ref, grid_ref, side_even_ref, side_odd_ref, even_ref, odd_ref, patch_ref, halo):
    s = pl.program_id(0)

    @pl.when(s == 0)
    def _():
        assemble(meta_ref, grid_ref, side_even_ref, side_odd_ref, halo, (even_ref, odd_ref))

    pos = pos_ref[s]

    @pl.when(pos >= 0)
    def _():
        build_patches(pos, halo, patch_ref)


def weight_kernel(pos_ref, meta_ref, grid_ref, side_even_ref, side_odd_ref, xt_ref, patch_ref, total, halo):
    s = pl.program_id(0)

    @pl.when(s == 0)
    def _():
        assemble(meta_ref, grid_ref, side_even_ref, side_odd_ref, halo)

        def clear(o, carry):
            total[pl.ds(pl.multiple_of(o * CH, CH), CH)] = jnp.zeros((CH, CH), F32)
            return carry

        lax.fori_loop(0, OFFSETS + 1, clear, 0)

    pos = pos_ref[s]

    @pl.when(pos >= 0)
    def _():
        build_patches(pos, halo, patch_ref)
        for p in range(3):
            terms = jnp.dot(xt_ref[0], patch_rows(patch_ref, p), preferred_element_type=F32)
            for k in range(9):
                row = (OFFSETS - 1 - (p * 9 + k)) * CH
                total[row : row + CH] += terms[:, k * CH : (k + 1) * CH]


def rim_kernel(pos_ref, meta_ref, even_ref, odd_ref, xt_ref, total_ref, patch_in, patch_out, keep_ref, send_ref, rims, rows, total, sems):
    core, own, other, odd_x = meta_ref[0], meta_ref[1], meta_ref[2], meta_ref[3]
    for i, ref in enumerate((even_ref, odd_ref)):
        at = 1 - odd_x if i == 0 else odd_x
        for r, a in enumerate(shifted(ref[...])):
            for bz in range(2):
                rims[at, r, bz] = a[:, bz]

    def clear(o, carry):
        at = pl.ds(pl.multiple_of(o * CH, CH), CH)
        total[at] = total_ref[at]
        return carry

    lax.fori_loop(0, OFFSETS + 1, clear, 0)

    def store(s, end):
        return pltpu.make_async_copy(rows.at[s], patch_out.at[s, 9 * end], sems.at[s])

    for s in range(SLOTS):
        pos = pos_ref[s]
        for end, edge in ((0, 0), (1, 3)):

            @pl.when((pos >= 0) & ((pos >> 2) == edge))
            def _():
                _, by, bz = brick_of(pos)
                for r in range(3):
                    part = rims[end, r, bz, pl.ds(by * 8, 10)]
                    rows[s, :, r * CH : (r + 1) * CH] = part.reshape(PROWS, CH).astype(BF16)
                store(s, end).start()
                patch = jnp.concatenate([rows[s, pl.ds(q * 8, 64)] for q in range(3)], axis=1)
                blank = jnp.zeros_like(patch)
                if end == 0:
                    left, right = xt_ref[s, :, :CH], jnp.concatenate([patch, blank], axis=0)
                else:
                    left, right = xt_ref[s, :, VOX - CH :], jnp.concatenate([blank, patch], axis=0)
                terms = jnp.dot(left, right, preferred_element_type=F32)
                for k in range(9):
                    row = (OFFSETS - 1 - (18 * end + k)) * CH
                    total[row : row + CH] += terms[:, k * CH : (k + 1) * CH]

    def emit(j, carry):
        at = pl.multiple_of((core * BLOCKS + (j ^ own)) * BROWS, 8)
        keep_ref[j] = total[pl.ds(at, BROWS)]
        at = pl.multiple_of(((1 - core) * BLOCKS + (j ^ other)) * BROWS, 8)
        send_ref[j] = total[pl.ds(at, BROWS)]
        return carry

    lax.fori_loop(0, BLOCKS, emit, 0)
    for s in range(SLOTS):
        pos = pos_ref[s]
        for end, edge in ((0, 0), (1, 3)):

            @pl.when((pos >= 0) & ((pos >> 2) == edge))
            def _():
                store(s, end).wait()


PATCH_SHAPE = pltpu.HBM((SLOTS, 10, PROWS, 3 * CH), BF16)
PATCH_SPEC = pl.BlockSpec((1, 10, PROWS, 3 * CH), lambda s, *_: (s, 0, 0, 0))
HALO = pltpu.VMEM((3, 2, NX + 2, NY + 2, 8, CH), F32)
TOTAL = pltpu.VMEM(((OFFSETS + 1) * CH, CH), F32)


def patches(slot_pos, meta, grid, sides, planes):
    return pl.pallas_call(
        patches_kernel,
        out_shape=PATCH_SHAPE,
        grid=(SLOTS,),
        in_specs=[SMEM, SMEM] + [VMEM] * 5,
        out_specs=PATCH_SPEC,
        scratch_shapes=[HALO],
        compiler_params=pltpu.CompilerParams(vmem_limit_bytes=28 << 20),
        cost_estimate=pl.CostEstimate(flops=0, bytes_accessed=20 << 20, transcendentals=0),
        name="patches",
    )(slot_pos, meta, grid, *sides, *planes)


def weight_gradient(slot_pos, meta, grid, sides, xt):
    return pl.pallas_call(
        weight_kernel,
        out_shape=(PATCH_SHAPE, TOTAL),
        grid=(SLOTS,),
        in_specs=[SMEM, SMEM] + [VMEM] * 3 + [pl.BlockSpec((1, CH, VOX), lambda s: (s, 0, 0))],
        out_specs=(PATCH_SPEC, VMEM),
        scratch_shapes=[HALO],
        compiler_params=pltpu.CompilerParams(vmem_limit_bytes=30 << 20),
        cost_estimate=pl.CostEstimate(flops=2 * 4096 * OFFSETS * CH * CH, bytes_accessed=20 << 20, transcendentals=0),
        name="weight_gradient",
    )(slot_pos, meta, grid, *sides, xt)


def rim_terms(slot_pos, meta, planes, xt, total, patch):
    half = pltpu.VMEM((BLOCKS, BROWS, CH), F32)
    hbm = pl.BlockSpec(memory_space=pltpu.HBM)
    return pl.pallas_call(
        rim_kernel,
        out_shape=(PATCH_SHAPE, half, half),
        in_specs=[SMEM, SMEM] + [VMEM] * 4 + [hbm],
        out_specs=(hbm, VMEM, VMEM),
        input_output_aliases={6: 0},
        scratch_shapes=[
            pltpu.VMEM((2, 3, 2, NY + 2, 8, CH), F32),
            pltpu.VMEM((SLOTS, PROWS, 3 * CH), BF16),
            TOTAL,
            pltpu.SemaphoreType.DMA((SLOTS,)),
        ],
        compiler_params=pltpu.CompilerParams(vmem_limit_bytes=20 << 20),
        name="rim_terms",
    )(slot_pos, meta, *planes, xt, total, patch)


def conv_kernel(first, pos_ref, occ_ref, patch_ref, w_ref, *rest):
    out_ref = rest[-1]
    s = first + pl.program_id(0)
    pos = pos_ref[s]

    @pl.when(pos >= 0)
    def _():
        columns = mask_columns(occ_ref)
        total = jnp.dot(patch_rows(patch_ref, 0), w_ref[:KROW], preferred_element_type=F32)
        for p in range(1, 3):
            total += jnp.dot(patch_rows(patch_ref, p), w_ref[p * KROW : (p + 1) * KROW], preferred_element_type=F32)
        lane = lax.broadcasted_iota(jnp.int32, columns.shape, 1)
        keep = jnp.sum(jnp.where(lane == s, columns, 0.0), axis=1, keepdims=True)
        out_ref[0] = jnp.where(jnp.broadcast_to(keep, (VOX, CH)) > 0.5, total, 0.0).astype(BF16)

    @pl.when(pos < 0)
    def _():
        out_ref[0] = jnp.zeros((VOX, CH), BF16)


def convolve(slot_pos, occupancy, patch, weights, out, first, count):
    aliased = {} if out is None else {4: 0}
    extra = () if out is None else (out,)
    return pl.pallas_call(
        lambda *refs: conv_kernel(first, *refs),
        out_shape=jax.ShapeDtypeStruct((SLOTS, VOX, CH), BF16),
        grid=(count,),
        in_specs=[SMEM, VMEM, pl.BlockSpec((1, 10, PROWS, 3 * CH), lambda i: (first + i, 0, 0, 0)), VMEM]
        + [pl.BlockSpec(memory_space=pl.ANY)] * len(extra),
        out_specs=pl.BlockSpec((1, VOX, CH), lambda i: (first + i, 0, 0)),
        input_output_aliases=aliased,
        compiler_params=pltpu.CompilerParams(vmem_limit_bytes=16 << 20),
        cost_estimate=pl.CostEstimate(flops=count * 4 * VOX * OFFSETS * CH * CH, bytes_accessed=count << 20, transcendentals=0),
        name="convolve",
    )(slot_pos, occupancy, pin(patch, pltpu.HBM), weights, *extra)


def finish_kernel(meta_ref, own_ref, other_ref, out_ref, rows):
    core, own, other = meta_ref[0], meta_ref[1], meta_ref[2]

    def place_block(j, carry):
        at = pl.multiple_of((core * BLOCKS + (j ^ own)) * BROWS, 8)
        rows[pl.ds(at, BROWS)] = own_ref[j]
        at = pl.multiple_of(((1 - core) * BLOCKS + (j ^ other)) * BROWS, 8)
        rows[pl.ds(at, BROWS)] = other_ref[j]
        return carry

    lax.fori_loop(0, BLOCKS, place_block, 0)
    scale = 1.0 / math.sqrt(float(256 * SLOTS * VOX))

    def emit(o, carry):
        out_ref[o] = rows[pl.ds(pl.multiple_of(o * CH, CH), CH)] * scale
        return carry

    lax.fori_loop(0, OFFSETS, emit, 0)


def finish(meta, own, other):
    return pl.pallas_call(
        finish_kernel,
        out_shape=jax.ShapeDtypeStruct((OFFSETS, CH, CH), F32),
        in_specs=[SMEM, VMEM, VMEM],
        out_specs=VMEM,
        scratch_shapes=[pltpu.VMEM(((OFFSETS + 1) * CH, CH), F32)],
        compiler_params=pltpu.CompilerParams(vmem_limit_bytes=24 << 20),
        name="finish",
    )(meta, own, other)


def make_shards(sizes):
    everyone = list(itertools.product(*[range(n) for n in sizes]))
    n_y_lo, n_core = sizes[3], sizes[4]
    narrow = n_y_lo * n_core
    wide = len(everyone) // narrow

    def number(at):
        flat = 0
        for a, n in zip(at, sizes):
            flat = flat * n + a
        return flat

    def mate(at, axis, k):
        y_hi, z, x, y_lo, core = at
        if isinstance(axis, tuple):
            axis = axis[core]
        y = y_hi * n_y_lo + y_lo
        if axis == "core":
            core ^= k
        elif axis == "x":
            x ^= k
        elif axis == "y":
            y ^= k
        else:
            z ^= k
        return (y // n_y_lo, z, x, y % n_y_lo, core)

    def swap(value, axis, k):
        return lax.ppermute(value, AXES, [(number(a), number(mate(a, axis, k))) for a in everyone])

    def exchange_wide(value, start):
        pairs = [(i * narrow + j, k * narrow + j) for a in range(start, wide - 1, 2) for i, k in ((a, a + 1), (a + 1, a)) for j in range(narrow)]
        return lax.ppermute(value, AXES, pairs)

    def exchange_narrow(value, start):
        pairs = [(i * narrow + j, i * narrow + k) for i in range(wide) for a in range(start, narrow - 1, 2) for j, k in ((a, a + 1), (a + 1, a))]
        return lax.ppermute(value, AXES, pairs)

    first, second = ("y", "x"), ("x", "y")

    def tie(*values):
        return lax.optimization_barrier(values)

    def scatter(value, axis):
        n = value.shape[0] // 4
        return [swap(value[k * n : (k + 1) * n], axis, k) for k in (2, 1, 3)]

    def add(value, parts):
        total = value[: parts[0].shape[0]]
        for part in parts:
            total = total + part
        return total

    def copies(value, axis, ks):
        return [swap(value, axis, k) for k in ks]

    def join(value, parts):
        return jnp.concatenate([value, parts[1], parts[0], parts[2]], axis=0)

    def shards(features, weights, cotangent, occupancy, slot_pos):
        core = lax.axis_index("core")
        x_at = lax.axis_index("x")
        y_at = lax.axis_index("y_hi") * n_y_lo + lax.axis_index("y_lo")
        yx, xy = y_at * 4 + x_at, x_at * 4 + y_at
        odd_x = x_at & 1
        meta = jnp.stack([core, jnp.where(core == 0, yx, xy), jnp.where(core == 0, xy, yx), odd_x]).astype(jnp.int32)
        xg, cg, xt, even, odd, side_even, side_odd = place(slot_pos, meta, occupancy, features, cotangent)
        side_even, side_odd, source = tie(side_even, side_odd, weights)
        side_even = exchange_narrow(side_even, 0)
        side_odd = exchange_narrow(side_odd, 1)
        w_backward = source[::-1].transpose(0, 2, 1).reshape(OFFSETS * CH, CH)
        side_even, side_odd, w_backward = tie(side_even, side_odd, w_backward)
        y_before, y_after = jnp.where(core == 0, side_odd, side_even), jnp.where(core == 0, side_even, side_odd)

        def rim(plane, last):
            ends = [jnp.where(last, v[:, NX - 1 :], v[:, :1]) for v in (y_before, y_after)]
            return jnp.concatenate([ends[0], plane, ends[1]], axis=1)

        even, odd, pos = tie(rim(even, odd_x == 0), rim(odd, odd_x == 1), slot_pos)
        even = exchange_wide(even, 0)
        odd = exchange_wide(odd, 1)
        cot_patch, total = weight_gradient(pos, meta, cg, (side_even[0], side_odd[0]), xt)
        even, odd, total = tie(even, odd, total)
        cot_patch, keep, send = rim_terms(slot_pos, meta, (even[0], odd[0]), xt, total, cot_patch)
        w_forward = weights.reshape(OFFSETS * CH, CH)
        done = {"outputs": None, "grad_input": None, "patch": None}

        def backward(at, pos):
            done["grad_input"] = convolve(pos, occupancy, cot_patch, w_backward, done["grad_input"], *at)
            return "grad_input"

        def forward(at, pos):
            done["outputs"] = convolve(pos, occupancy, done["patch"], w_forward, done["outputs"], *at)
            return "outputs"

        def gather_patches(at, pos):
            done["patch"] = patches(pos, meta, xg, (side_even[1], side_odd[1]), (even[1], odd[1]))
            return "patch"

        def stage(value, start, *work):
            value, pos = tie(value, slot_pos)
            parts = start(value)
            names = {call(at, pos) for call, at in work}
            held = tie(parts, *[done[n] for n in sorted(names)])
            for n, v in zip(sorted(names), held[1:]):
                done[n] = v
            return value, held[0]

        _, (got,) = stage(send, lambda v: copies(v, "core", (1,)), (backward, (0, 1)))
        total = keep + got
        total = add(*stage(total, lambda v: scatter(v, first), (backward, (1, 4))))
        total = add(*stage(total, lambda v: scatter(v, second), (backward, (5, 2))))
        total = add(*stage(total, lambda v: copies(v, "z", (2, 1, 3)), (gather_patches, None)))
        total = add(*stage(total, lambda v: copies(v, "z", (4,)), (backward, (7, 1)), (forward, (0, 1))))
        total = join(*stage(total, lambda v: copies(v, second, (2, 1, 3)), (forward, (1, 2))))
        total = join(*stage(total, lambda v: copies(v, first, (2, 1, 3)), (forward, (3, 4))))
        total, (got,) = stage(total, lambda v: copies(v, "core", (1,)), (forward, (7, 1)))
        grad_weight = finish(meta, total, got)
        return done["outputs"], done["grad_input"], grad_weight

    return shards


def solution(mesh):
    sizes = (2, 8, 4, 2, 2)
    fine = Mesh(mesh.devices.reshape(sizes), AXES)
    return jax.shard_map(
        make_shards(sizes),
        mesh=fine,
        in_specs=(P(AXES, None, None), P(), P(AXES, None, None), P(AXES, None), P(AXES)),
        out_specs=(P(AXES, None, None), P(AXES, None, None), P()),
        check_vma=False,
    )
```

```python
import itertools
import math

import jax
import jax.numpy as jnp
from jax import lax
from jax.experimental import pallas as pl
from jax.experimental.pallas import tpu as pltpu
from jax.sharding import Mesh, PartitionSpec as P

AXES = ("y_hi", "z", "x", "y_lo", "core")
SLOTS = 8
VOX = 512
CH = 128
NX, NY, NZ = 32, 16, 16
OFFSETS = 27
KROW = 9 * CH
BLOCKS = 16
BROWS = 112
PROWS = 80
F32 = jnp.float32
BF16 = jnp.bfloat16
VMEM = pl.BlockSpec(memory_space=pltpu.VMEM)
SMEM = pl.BlockSpec(memory_space=pltpu.SMEM)
HBM = pl.BlockSpec(memory_space=pltpu.HBM)


def pin(value, space):
    return pltpu.with_memory_space_constraint(value, space)


def brick_of(pos):
    return pos >> 2, (pos >> 1) & 1, pos & 1


def mask_columns(occ_ref):
    return jnp.where(occ_ref[...] == 1, 1.0, 0.0).astype(F32).T


def place_kernel(pos_ref, meta_ref, occ_hbm, feat_hbm, cot_hbm, xg_hbm, cg_hbm, xt_hbm, even_ref, odd_ref, side_even_ref, side_odd_ref, occ, cells, slots, grids, xt, load_sems, grid_sems, xt_sem, occ_sem):
    def load(t, s):
        return pltpu.make_async_copy((cot_hbm, feat_hbm)[t].at[s], slots.at[t, s], load_sems.at[t, s])

    def save(t, n):
        part = pl.ds(n * 8, 8)
        return pltpu.make_async_copy(grids.at[t, part], (cg_hbm, xg_hbm)[t].at[part], grid_sems.at[t, n])

    load_occ = pltpu.make_async_copy(occ_hbm, occ, occ_sem)
    load_occ.start()
    for t in range(2):
        for s in range(SLOTS):
            load(t, s).start()
    core, odd_x = meta_ref[0], meta_ref[3]
    for t in range(2):

        def clear(x, carry):
            cells[x] = jnp.zeros((NY, 2, 8, CH), F32)
            return carry

        lax.fori_loop(0, NX, clear, 0)
        if t == 0:
            load_occ.wait()
            columns = mask_columns(occ)
        for s in range(SLOTS):
            load(t, s).wait()
            pos = pos_ref[s]

            @pl.when(pos >= 0)
            def _():
                bx, by, bz = brick_of(pos)
                keep = jnp.broadcast_to(columns[:, s : s + 1], (VOX, CH))
                value = jnp.where(keep > 0.5, slots[t, s].astype(F32), 0.0)
                cells[pl.ds(bx * 8, 8), pl.ds(by * 8, 8), bz] = value.reshape(8, 8, 8, CH)
                if t == 1:
                    xt[s] = value.T.astype(BF16)

        if t == 1:
            save_xt = pltpu.make_async_copy(xt, xt_hbm, xt_sem)
            save_xt.start()

        def emit(x, carry):
            grids[t, x] = cells[x].reshape(NY, NZ, CH).astype(BF16)
            return carry

        for n in range(4):
            lax.fori_loop(n * 8, n * 8 + 8, emit, 0)
            save(t, n).start()
        even_ref[t] = grids[t, (NX - 1) * (1 - odd_x)]
        odd_ref[t] = grids[t, (NX - 1) * odd_x]
        side_even_ref[t] = grids[t, :, (NY - 1) * (1 - core)]
        side_odd_ref[t] = grids[t, :, (NY - 1) * core]
    save_xt.wait()
    for t in range(2):
        for n in range(4):
            save(t, n).wait()


def place(slot_pos, meta, occupancy, features, cotangent):
    plane = jax.ShapeDtypeStruct((2, NY, NZ, CH), BF16)
    side = jax.ShapeDtypeStruct((2, NX, NZ, CH), BF16)
    grid = pltpu.HBM((NX, NY, NZ, CH), BF16)
    hbm = pl.BlockSpec(memory_space=pltpu.HBM)
    return pl.pallas_call(
        place_kernel,
        out_shape=(grid, grid, pltpu.HBM((SLOTS, CH, VOX), BF16), plane, plane, side, side),
        in_specs=[SMEM, SMEM, hbm, hbm, hbm],
        out_specs=(hbm,) * 3 + (VMEM,) * 4,
        scratch_shapes=[
            pltpu.VMEM((SLOTS, VOX), jnp.int32),
            pltpu.VMEM((NX, NY, 2, 8, CH), F32),
            pltpu.VMEM((2, SLOTS, VOX, CH), BF16),
            pltpu.VMEM((2, NX, NY, NZ, CH), BF16),
            pltpu.VMEM((SLOTS, CH, VOX), BF16),
            pltpu.SemaphoreType.DMA((2, SLOTS)),
            pltpu.SemaphoreType.DMA((2, 4)),
            pltpu.SemaphoreType.DMA,
            pltpu.SemaphoreType.DMA,
        ],
        compiler_params=pltpu.CompilerParams(vmem_limit_bytes=24 << 20),
        name="place",
    )(slot_pos, meta, *[pin(a, pltpu.HBM) for a in (occupancy, features, cotangent)])


def shifted(v):
    n = v.shape[0]
    flat = v.astype(F32).reshape(n * NZ, CH)
    z = lax.broadcasted_iota(jnp.int32, flat.shape, 0) & (NZ - 1)
    back = jnp.where(z == 0, 0.0, pltpu.roll(flat, 1, axis=0))
    ahead = jnp.where(z == NZ - 1, 0.0, pltpu.roll(flat, n * NZ - 1, axis=0))
    return [a.reshape(n, 2, 8, CH) for a in (back, flat, ahead)]


def assemble(meta_ref, t, grid_hbm, side_even_ref, side_odd_ref, halo, cells, sems, planes=None):
    core, odd_x = meta_ref[0], meta_ref[3]

    def load(n):
        part = pl.ds(n * 8, 8)
        return pltpu.make_async_copy(grid_hbm.at[part], cells.at[part], sems.at[n])

    for n in range(4):
        load(n).start()

    def body(x, carry):
        for r, a in enumerate(shifted(cells[x])):
            for bz in range(2):
                halo[r, bz, x + 1, pl.ds(1, NY)] = a[:, bz]
        return carry

    for y, ref in (((NY + 1) * (1 - core), side_even_ref), ((NY + 1) * core, side_odd_ref)):
        for r, a in enumerate(shifted(ref[t])):
            for bz in range(2):
                halo[r, bz, pl.ds(1, NX), y] = a[:, bz]
    for i, x in enumerate(((NX + 1) * (1 - odd_x), (NX + 1) * odd_x)):
        if planes is None:
            halo[:, :, x] = jnp.zeros((3, 2, NY + 2, 8, CH), F32)
        else:
            for r, a in enumerate(shifted(planes[i][t])):
                for bz in range(2):
                    halo[r, bz, x] = a[:, bz]
    for n in range(4):
        load(n).wait()
        lax.fori_loop(n * 8, n * 8 + 8, body, 0)


def build_patches(pos, halo, patch_ref):
    bx, by, bz = brick_of(pos)
    for x in range(10):
        for r in range(3):
            rows = halo[r, bz, bx * 8 + x, pl.ds(by * 8, 10)]
            patch_ref[0, x, :, r * CH : (r + 1) * CH] = rows.reshape(PROWS, CH).astype(BF16)


def patch_rows(patch_ref, p):
    parts = [patch_ref[0, pl.ds(p, 8), pl.ds(q * 8, 64)].reshape(VOX, 3 * CH) for q in range(3)]
    return jnp.concatenate(parts, axis=1)


def patches_kernel(pos_ref, meta_ref, grid_hbm, side_even_ref, side_odd_ref, even_ref, odd_ref, patch_ref, halo, cells, sems):
    s = pl.program_id(0)

    @pl.when(s == 0)
    def _():
        assemble(meta_ref, 1, grid_hbm, side_even_ref, side_odd_ref, halo, cells, sems, (even_ref, odd_ref))

    pos = pos_ref[s]

    @pl.when(pos >= 0)
    def _():
        build_patches(pos, halo, patch_ref)


def weight_kernel(pos_ref, meta_ref, grid_hbm, side_even_ref, side_odd_ref, xt_ref, patch_ref, total, halo, cells, sems):
    s = pl.program_id(0)

    @pl.when(s == 0)
    def _():
        assemble(meta_ref, 0, grid_hbm, side_even_ref, side_odd_ref, halo, cells, sems)

        def clear(o, carry):
            total[pl.ds(pl.multiple_of(o * CH, CH), CH)] = jnp.zeros((CH, CH), F32)
            return carry

        lax.fori_loop(0, OFFSETS + 1, clear, 0)

    pos = pos_ref[s]

    @pl.when(pos >= 0)
    def _():
        build_patches(pos, halo, patch_ref)
        for p in range(3):
            terms = jnp.dot(xt_ref[0], patch_rows(patch_ref, p), preferred_element_type=F32)
            for k in range(9):
                row = (OFFSETS - 1 - (p * 9 + k)) * CH
                total[row : row + CH] += terms[:, k * CH : (k + 1) * CH]


def rim_kernel(pos_ref, meta_ref, even_ref, odd_ref, xt_ref, total_ref, patch_in, patch_out, keep_ref, send_ref, rims, rows, total, sems):
    core, own, other, odd_x = meta_ref[0], meta_ref[1], meta_ref[2], meta_ref[3]
    for i, ref in enumerate((even_ref, odd_ref)):
        at = 1 - odd_x if i == 0 else odd_x
        for r, a in enumerate(shifted(ref[0])):
            for bz in range(2):
                rims[at, r, bz] = a[:, bz]

    def clear(o, carry):
        at = pl.ds(pl.multiple_of(o * CH, CH), CH)
        total[at] = total_ref[at]
        return carry

    lax.fori_loop(0, OFFSETS + 1, clear, 0)

    def store(s, end):
        return pltpu.make_async_copy(rows.at[s], patch_out.at[s, 9 * end], sems.at[s])

    for s in range(SLOTS):
        pos = pos_ref[s]
        for end, edge in ((0, 0), (1, 3)):

            @pl.when((pos >= 0) & ((pos >> 2) == edge))
            def _():
                _, by, bz = brick_of(pos)
                for r in range(3):
                    part = rims[end, r, bz, pl.ds(by * 8, 10)]
                    rows[s, :, r * CH : (r + 1) * CH] = part.reshape(PROWS, CH).astype(BF16)
                store(s, end).start()
                patch = jnp.concatenate([rows[s, pl.ds(q * 8, 64)] for q in range(3)], axis=1)
                blank = jnp.zeros_like(patch)
                if end == 0:
                    left, right = xt_ref[s, :, :CH], jnp.concatenate([patch, blank], axis=0)
                else:
                    left, right = xt_ref[s, :, VOX - CH :], jnp.concatenate([blank, patch], axis=0)
                terms = jnp.dot(left, right, preferred_element_type=F32)
                for k in range(9):
                    row = (OFFSETS - 1 - (18 * end + k)) * CH
                    total[row : row + CH] += terms[:, k * CH : (k + 1) * CH]

    def emit(j, carry):
        at = pl.multiple_of((core * BLOCKS + (j ^ own)) * BROWS, 8)
        keep_ref[j] = total[pl.ds(at, BROWS)]
        at = pl.multiple_of(((1 - core) * BLOCKS + (j ^ other)) * BROWS, 8)
        send_ref[j] = total[pl.ds(at, BROWS)]
        return carry

    lax.fori_loop(0, BLOCKS, emit, 0)
    for s in range(SLOTS):
        pos = pos_ref[s]
        for end, edge in ((0, 0), (1, 3)):

            @pl.when((pos >= 0) & ((pos >> 2) == edge))
            def _():
                store(s, end).wait()


PATCH_SHAPE = pltpu.HBM((SLOTS, 10, PROWS, 3 * CH), BF16)
PATCH_SPEC = pl.BlockSpec((1, 10, PROWS, 3 * CH), lambda s, *_: (s, 0, 0, 0))
HALO = pltpu.VMEM((3, 2, NX + 2, NY + 2, 8, CH), F32)
TOTAL = pltpu.VMEM(((OFFSETS + 1) * CH, CH), F32)


def patches(slot_pos, meta, grid, sides, planes):
    return pl.pallas_call(
        patches_kernel,
        out_shape=PATCH_SHAPE,
        grid=(SLOTS,),
        in_specs=[SMEM, SMEM, HBM] + [VMEM] * 4,
        out_specs=PATCH_SPEC,
        scratch_shapes=[HALO, pltpu.VMEM((NX, NY, NZ, CH), BF16), pltpu.SemaphoreType.DMA((4,))],
        compiler_params=pltpu.CompilerParams(vmem_limit_bytes=28 << 20),
        cost_estimate=pl.CostEstimate(flops=0, bytes_accessed=20 << 20, transcendentals=0),
        name="patches",
    )(slot_pos, meta, pin(grid, pltpu.HBM), *sides, *planes)


def weight_gradient(slot_pos, meta, grid, sides, xt):
    return pl.pallas_call(
        weight_kernel,
        out_shape=(PATCH_SHAPE, TOTAL),
        grid=(SLOTS,),
        in_specs=[SMEM, SMEM, HBM] + [VMEM] * 2 + [pl.BlockSpec((1, CH, VOX), lambda s: (s, 0, 0))],
        out_specs=(PATCH_SPEC, VMEM),
        scratch_shapes=[HALO, pltpu.VMEM((NX, NY, NZ, CH), BF16), pltpu.SemaphoreType.DMA((4,))],
        compiler_params=pltpu.CompilerParams(vmem_limit_bytes=30 << 20),
        cost_estimate=pl.CostEstimate(flops=2 * 4096 * OFFSETS * CH * CH, bytes_accessed=20 << 20, transcendentals=0),
        name="weight_gradient",
    )(slot_pos, meta, pin(grid, pltpu.HBM), *sides, xt)


def rim_terms(slot_pos, meta, planes, xt, total, patch):
    half = pltpu.VMEM((BLOCKS, BROWS, CH), F32)
    hbm = pl.BlockSpec(memory_space=pltpu.HBM)
    return pl.pallas_call(
        rim_kernel,
        out_shape=(PATCH_SHAPE, half, half),
        in_specs=[SMEM, SMEM] + [VMEM] * 4 + [hbm],
        out_specs=(hbm, VMEM, VMEM),
        input_output_aliases={6: 0},
        scratch_shapes=[
            pltpu.VMEM((2, 3, 2, NY + 2, 8, CH), F32),
            pltpu.VMEM((SLOTS, PROWS, 3 * CH), BF16),
            TOTAL,
            pltpu.SemaphoreType.DMA((SLOTS,)),
        ],
        compiler_params=pltpu.CompilerParams(vmem_limit_bytes=20 << 20),
        name="rim_terms",
    )(slot_pos, meta, *planes, xt, total, patch)


def flip_kernel(w_ref, out_ref):
    for o in range(OFFSETS):
        out_ref[o * CH : (o + 1) * CH] = w_ref[OFFSETS - 1 - o].T


def flip(weights):
    return pl.pallas_call(
        flip_kernel,
        out_shape=pltpu.VMEM((OFFSETS * CH, CH), BF16),
        in_specs=[VMEM],
        out_specs=VMEM,
        compiler_params=pltpu.CompilerParams(vmem_limit_bytes=8 << 20),
        cost_estimate=pl.CostEstimate(flops=0, bytes_accessed=2 << 20, transcendentals=0),
        name="flip",
    )(weights)


def conv_kernel(first, pos_ref, occ_ref, patch_ref, w_ref, *rest):
    out_ref = rest[-1]
    s = first + pl.program_id(0)
    pos = pos_ref[s]

    @pl.when(pos >= 0)
    def _():
        columns = mask_columns(occ_ref)
        total = jnp.dot(patch_rows(patch_ref, 0), w_ref[:KROW], preferred_element_type=F32)
        for p in range(1, 3):
            total += jnp.dot(patch_rows(patch_ref, p), w_ref[p * KROW : (p + 1) * KROW], preferred_element_type=F32)
        lane = lax.broadcasted_iota(jnp.int32, columns.shape, 1)
        keep = jnp.sum(jnp.where(lane == s, columns, 0.0), axis=1, keepdims=True)
        out_ref[0] = jnp.where(jnp.broadcast_to(keep, (VOX, CH)) > 0.5, total, 0.0).astype(BF16)

    @pl.when(pos < 0)
    def _():
        out_ref[0] = jnp.zeros((VOX, CH), BF16)


def convolve(slot_pos, occupancy, patch, weights, out, first, count):
    aliased = {} if out is None else {4: 0}
    extra = () if out is None else (out,)
    return pl.pallas_call(
        lambda *refs: conv_kernel(first, *refs),
        out_shape=jax.ShapeDtypeStruct((SLOTS, VOX, CH), BF16),
        grid=(count,),
        in_specs=[SMEM, VMEM, pl.BlockSpec((1, 10, PROWS, 3 * CH), lambda i: (first + i, 0, 0, 0)), VMEM]
        + [pl.BlockSpec(memory_space=pl.ANY)] * len(extra),
        out_specs=pl.BlockSpec((1, VOX, CH), lambda i: (first + i, 0, 0)),
        input_output_aliases=aliased,
        compiler_params=pltpu.CompilerParams(vmem_limit_bytes=16 << 20),
        cost_estimate=pl.CostEstimate(flops=count * 4 * VOX * OFFSETS * CH * CH, bytes_accessed=count << 20, transcendentals=0),
        name="convolve",
    )(slot_pos, occupancy, pin(patch, pltpu.HBM), pin(weights, pltpu.VMEM), *extra)


def finish_kernel(meta_ref, own_ref, other_ref, out_ref, rows):
    core, own, other = meta_ref[0], meta_ref[1], meta_ref[2]

    def place_block(j, carry):
        at = pl.multiple_of((core * BLOCKS + (j ^ own)) * BROWS, 8)
        rows[pl.ds(at, BROWS)] = own_ref[j]
        at = pl.multiple_of(((1 - core) * BLOCKS + (j ^ other)) * BROWS, 8)
        rows[pl.ds(at, BROWS)] = other_ref[j]
        return carry

    lax.fori_loop(0, BLOCKS, place_block, 0)
    scale = 1.0 / math.sqrt(float(256 * SLOTS * VOX))

    def emit(o, carry):
        out_ref[o] = rows[pl.ds(pl.multiple_of(o * CH, CH), CH)] * scale
        return carry

    lax.fori_loop(0, OFFSETS, emit, 0)


def finish(meta, own, other):
    return pl.pallas_call(
        finish_kernel,
        out_shape=jax.ShapeDtypeStruct((OFFSETS, CH, CH), F32),
        in_specs=[SMEM, VMEM, VMEM],
        out_specs=VMEM,
        scratch_shapes=[pltpu.VMEM(((OFFSETS + 1) * CH, CH), F32)],
        compiler_params=pltpu.CompilerParams(vmem_limit_bytes=24 << 20),
        name="finish",
    )(meta, own, other)


def make_shards(sizes):
    everyone = list(itertools.product(*[range(n) for n in sizes]))
    n_y_lo, n_core = sizes[3], sizes[4]
    narrow = n_y_lo * n_core
    wide = len(everyone) // narrow

    def number(at):
        flat = 0
        for a, n in zip(at, sizes):
            flat = flat * n + a
        return flat

    def mate(at, axis, k):
        y_hi, z, x, y_lo, core = at
        if isinstance(axis, tuple):
            axis = axis[core]
        y = y_hi * n_y_lo + y_lo
        if axis == "core":
            core ^= k
        elif axis == "x":
            x ^= k
        elif axis == "y":
            y ^= k
        else:
            z ^= k
        return (y // n_y_lo, z, x, y % n_y_lo, core)

    def swap(value, axis, k):
        return lax.ppermute(value, AXES, [(number(a), number(mate(a, axis, k))) for a in everyone])

    def exchange_wide(value, start):
        pairs = [(i * narrow + j, k * narrow + j) for a in range(start, wide - 1, 2) for i, k in ((a, a + 1), (a + 1, a)) for j in range(narrow) if a + 1 != wide // 2]
        return lax.ppermute(value, AXES, pairs)

    def exchange_far(value):
        a = wide // 2 - 1
        pairs = [(i * narrow + j, k * narrow + j) for i, k in ((a, a + 1), (a + 1, a)) for j in range(narrow)]
        return lax.ppermute(value, AXES, pairs)

    def exchange_narrow(value, start):
        pairs = [(i * narrow + j, i * narrow + k) for i in range(wide) for a in range(start, narrow - 1, 2) for j, k in ((a, a + 1), (a + 1, a))]
        return lax.ppermute(value, AXES, pairs)

    first, second = ("y", "x"), ("x", "y")

    def tie(*values):
        return lax.optimization_barrier(values)

    def scatter(value, axis):
        n = value.shape[0] // 4
        return [swap(value[k * n : (k + 1) * n], axis, k) for k in (2, 1, 3)]

    def add(value, parts):
        total = value[: parts[0].shape[0]]
        for part in parts:
            total = total + part
        return total

    def copies(value, axis, ks):
        return [swap(value, axis, k) for k in ks]

    def join(value, parts):
        return jnp.concatenate([value, parts[1], parts[0], parts[2]], axis=0)

    def shards(features, weights, cotangent, occupancy, slot_pos):
        slot_pos = pin(slot_pos, pltpu.HBM)
        core = lax.axis_index("core")
        x_at = lax.axis_index("x")
        y_at = lax.axis_index("y_hi") * n_y_lo + lax.axis_index("y_lo")
        yx, xy = y_at * 4 + x_at, x_at * 4 + y_at
        odd_x = x_at & 1
        meta = jnp.stack([core, jnp.where(core == 0, yx, xy), jnp.where(core == 0, xy, yx), odd_x]).astype(jnp.int32)
        xg, cg, xt, even, odd, side_even, side_odd = place(slot_pos, meta, occupancy, features, cotangent)
        side_even, side_odd, source = tie(side_even, side_odd, weights)
        side_even = exchange_narrow(side_even, 0)
        side_odd = exchange_narrow(side_odd, 1)
        side_even, side_odd, w_backward = tie(side_even, side_odd, flip(source))

        def rim(plane, last):
            ends = [jnp.where(last, v[:, NX - 1 :], v[:, :1]) for v in (side_even, side_odd)]
            first = core == 0
            return jnp.concatenate([jnp.where(first, ends[1], ends[0]), plane, jnp.where(first, ends[0], ends[1])], axis=1)

        even, odd = rim(even, odd_x == 0), rim(odd, odd_x == 1)
        far = exchange_far(odd)
        even, odd, pos = tie(even, odd, slot_pos)
        even = exchange_wide(even, 0)
        odd = exchange_wide(odd, 1)
        cot_patch, total = weight_gradient(pos, meta, cg, (side_even, side_odd), xt)
        even, odd, far, total = tie(even, odd, far, total)
        odd = odd + far
        cot_patch, keep, send = rim_terms(slot_pos, meta, (even, odd), xt, total, cot_patch)
        w_forward = weights.reshape(OFFSETS * CH, CH)
        done = {"outputs": None, "grad_input": None, "patch": None}

        def backward(at, pos):
            done["grad_input"] = convolve(pos, occupancy, cot_patch, w_backward, done["grad_input"], *at)
            return "grad_input"

        def forward(at, pos):
            done["outputs"] = convolve(pos, occupancy, done["patch"], w_forward, done["outputs"], *at)
            return "outputs"

        def gather_patches(at, pos):
            done["patch"] = patches(pos, meta, xg, (side_even, side_odd), (even, odd))
            return "patch"

        def stage(value, start, *work):
            value, pos = tie(value, slot_pos)
            parts = start(value)
            names = {call(at, pos) for call, at in work}
            held = tie(parts, *[done[n] for n in sorted(names)])
            for n, v in zip(sorted(names), held[1:]):
                done[n] = v
            return value, held[0]

        _, (got,) = stage(send, lambda v: copies(v, "core", (1,)), (backward, (0, 1)))
        total = keep + got
        total = add(*stage(total, lambda v: scatter(v, first), (backward, (1, 4))))
        total = add(*stage(total, lambda v: scatter(v, second), (backward, (5, 2))))
        total = add(*stage(total, lambda v: copies(v, "z", (2, 1, 3)), (gather_patches, None)))
        total = add(*stage(total, lambda v: copies(v, "z", (4,)), (backward, (7, 1)), (forward, (0, 1))))
        total = join(*stage(total, lambda v: copies(v, second, (2, 1, 3)), (forward, (1, 2))))
        total = join(*stage(total, lambda v: copies(v, first, (2, 1, 3)), (forward, (3, 4))))
        total, (got,) = stage(total, lambda v: copies(v, "core", (1,)), (forward, (7, 1)))
        grad_weight = finish(meta, total, got)
        return done["outputs"], done["grad_input"], grad_weight

    return shards


def solution(mesh):
    sizes = (2, 8, 4, 2, 2)
    fine = Mesh(mesh.devices.reshape(sizes), AXES)
    return jax.shard_map(
        make_shards(sizes),
        mesh=fine,
        in_specs=(P(AXES, None, None), P(), P(AXES, None, None), P(AXES, None), P(AXES)),
        out_specs=(P(AXES, None, None), P(AXES, None, None), P()),
        check_vma=False,
    )
```

```python
import itertools
import math

import jax
import jax.numpy as jnp
from jax import lax
from jax.experimental import pallas as pl
from jax.experimental.pallas import tpu as pltpu
from jax.sharding import Mesh, PartitionSpec as P

AXES = ("y_hi", "z", "x", "y_lo", "core")
SLOTS = 8
VOX = 512
CH = 128
NX, NY, NZ = 32, 16, 16
OFFSETS = 27
KROW = 9 * CH
BLOCKS = 16
BROWS = 112
PROWS = 80
F32 = jnp.float32
BF16 = jnp.bfloat16
VMEM = pl.BlockSpec(memory_space=pltpu.VMEM)
SMEM = pl.BlockSpec(memory_space=pltpu.SMEM)
HBM = pl.BlockSpec(memory_space=pltpu.HBM)


def pin(value, space):
    return pltpu.with_memory_space_constraint(value, space)


def brick_of(pos):
    return pos >> 2, (pos >> 1) & 1, pos & 1


def mask_columns(occ_ref):
    return jnp.where(occ_ref[...] == 1, 1.0, 0.0).astype(F32).T


def place_kernel(pos_ref, meta_ref, occ_hbm, feat_hbm, cot_hbm, xg_hbm, cg_hbm, xt_hbm, even_ref, odd_ref, side_even_ref, side_odd_ref, occ, cells, slots, grids, xt, load_sems, grid_sems, xt_sem, occ_sem):
    def load(t, s):
        return pltpu.make_async_copy((cot_hbm, feat_hbm)[t].at[s], slots.at[t, s], load_sems.at[t, s])

    def save(t, n):
        part = pl.ds(n * 8, 8)
        return pltpu.make_async_copy(grids.at[t, part], (cg_hbm, xg_hbm)[t].at[part], grid_sems.at[t, n])

    load_occ = pltpu.make_async_copy(occ_hbm, occ, occ_sem)
    load_occ.start()
    for t in range(2):
        for s in range(SLOTS):
            load(t, s).start()
    core, odd_x = meta_ref[0], meta_ref[3]
    for t in range(2):

        def clear(x, carry):
            cells[x] = jnp.zeros((NY, 2, 8, CH), F32)
            return carry

        lax.fori_loop(0, NX, clear, 0)
        if t == 0:
            load_occ.wait()
            columns = mask_columns(occ)
        for s in range(SLOTS):
            load(t, s).wait()
            pos = pos_ref[s]

            @pl.when(pos >= 0)
            def _():
                bx, by, bz = brick_of(pos)
                keep = jnp.broadcast_to(columns[:, s : s + 1], (VOX, CH))
                value = jnp.where(keep > 0.5, slots[t, s].astype(F32), 0.0)
                cells[pl.ds(bx * 8, 8), pl.ds(by * 8, 8), bz] = value.reshape(8, 8, 8, CH)
                if t == 1:
                    xt[s] = value.T.astype(BF16)

        if t == 1:
            save_xt = pltpu.make_async_copy(xt, xt_hbm, xt_sem)
            save_xt.start()

        def emit(x, carry):
            grids[t, x] = cells[x].reshape(NY, NZ, CH).astype(BF16)
            return carry

        for n in range(4):
            lax.fori_loop(n * 8, n * 8 + 8, emit, 0)
            save(t, n).start()
        even_ref[t] = grids[t, (NX - 1) * (1 - odd_x)]
        odd_ref[t] = grids[t, (NX - 1) * odd_x]
        side_even_ref[t] = grids[t, :, (NY - 1) * (1 - core)]
        side_odd_ref[t] = grids[t, :, (NY - 1) * core]
    save_xt.wait()
    for t in range(2):
        for n in range(4):
            save(t, n).wait()


def place(slot_pos, meta, occupancy, features, cotangent):
    plane = jax.ShapeDtypeStruct((2, NY, NZ, CH), BF16)
    side = jax.ShapeDtypeStruct((2, NX, NZ, CH), BF16)
    grid = pltpu.HBM((NX, NY, NZ, CH), BF16)
    hbm = pl.BlockSpec(memory_space=pltpu.HBM)
    return pl.pallas_call(
        place_kernel,
        out_shape=(grid, grid, pltpu.HBM((SLOTS, CH, VOX), BF16), plane, plane, side, side),
        in_specs=[SMEM, SMEM, hbm, hbm, hbm],
        out_specs=(hbm,) * 3 + (VMEM,) * 4,
        scratch_shapes=[
            pltpu.VMEM((SLOTS, VOX), jnp.int32),
            pltpu.VMEM((NX, NY, 2, 8, CH), F32),
            pltpu.VMEM((2, SLOTS, VOX, CH), BF16),
            pltpu.VMEM((2, NX, NY, NZ, CH), BF16),
            pltpu.VMEM((SLOTS, CH, VOX), BF16),
            pltpu.SemaphoreType.DMA((2, SLOTS)),
            pltpu.SemaphoreType.DMA((2, 4)),
            pltpu.SemaphoreType.DMA,
            pltpu.SemaphoreType.DMA,
        ],
        compiler_params=pltpu.CompilerParams(vmem_limit_bytes=24 << 20),
        name="place",
    )(slot_pos, meta, *[pin(a, pltpu.HBM) for a in (occupancy, features, cotangent)])


def shifted(v):
    n = v.shape[0]
    flat = v.astype(F32).reshape(n * NZ, CH)
    z = lax.broadcasted_iota(jnp.int32, flat.shape, 0) & (NZ - 1)
    back = jnp.where(z == 0, 0.0, pltpu.roll(flat, 1, axis=0))
    ahead = jnp.where(z == NZ - 1, 0.0, pltpu.roll(flat, n * NZ - 1, axis=0))
    return [a.reshape(n, 2, 8, CH) for a in (back, flat, ahead)]


def assemble(meta_ref, t, grid_hbm, side_even_ref, side_odd_ref, halo, cells, sems, planes=None):
    core, odd_x = meta_ref[0], meta_ref[3]

    def load(n):
        part = pl.ds(n * 8, 8)
        return pltpu.make_async_copy(grid_hbm.at[part], cells.at[part], sems.at[n])

    for n in range(4):
        load(n).start()

    def body(x, carry):
        for r, a in enumerate(shifted(cells[x])):
            for bz in range(2):
                halo[r, bz, x + 1, pl.ds(1, NY)] = a[:, bz]
        return carry

    for y, ref in (((NY + 1) * (1 - core), side_even_ref), ((NY + 1) * core, side_odd_ref)):
        for r, a in enumerate(shifted(ref[t])):
            for bz in range(2):
                halo[r, bz, pl.ds(1, NX), y] = a[:, bz]
    for i, x in enumerate(((NX + 1) * (1 - odd_x), (NX + 1) * odd_x)):
        if planes is None:
            halo[:, :, x] = jnp.zeros((3, 2, NY + 2, 8, CH), F32)
        else:
            for r, a in enumerate(shifted(planes[i][t])):
                for bz in range(2):
                    halo[r, bz, x] = a[:, bz]
    for n in range(4):
        load(n).wait()
        lax.fori_loop(n * 8, n * 8 + 8, body, 0)


def build_patches(s, pos, halo, patch_ref):
    bx, by, bz = brick_of(pos)
    for x in range(10):
        for r in range(3):
            rows = halo[r, bz, bx * 8 + x, pl.ds(by * 8, 10)]
            patch_ref[s, x, :, r * CH : (r + 1) * CH] = rows.reshape(PROWS, CH).astype(BF16)


def patch_rows(patch_ref, s, p):
    parts = [patch_ref[s, pl.ds(p, 8), pl.ds(q * 8, 64)].reshape(VOX, 3 * CH) for q in range(3)]
    return jnp.concatenate(parts, axis=1)


def patches_kernel(pos_ref, meta_ref, grid_hbm, side_even_ref, side_odd_ref, even_ref, odd_ref, patch_ref, halo, cells, sems):
    s = pl.program_id(0)

    @pl.when(s == 0)
    def _():
        assemble(meta_ref, 1, grid_hbm, side_even_ref, side_odd_ref, halo, cells, sems, (even_ref, odd_ref))

    pos = pos_ref[s]

    @pl.when(pos >= 0)
    def _():
        build_patches(s, pos, halo, patch_ref)


def weight_kernel(pos_ref, meta_ref, grid_hbm, side_even_ref, side_odd_ref, xt_ref, patch_ref, total, halo, cells, sems):
    s = pl.program_id(0)

    @pl.when(s == 0)
    def _():
        assemble(meta_ref, 0, grid_hbm, side_even_ref, side_odd_ref, halo, cells, sems)

        def clear(o, carry):
            total[pl.ds(pl.multiple_of(o * CH, CH), CH)] = jnp.zeros((CH, CH), F32)
            return carry

        lax.fori_loop(0, OFFSETS + 1, clear, 0)

    pos = pos_ref[s]

    @pl.when(pos >= 0)
    def _():
        build_patches(s, pos, halo, patch_ref)
        for p in range(3):
            terms = jnp.dot(xt_ref[0], patch_rows(patch_ref, s, p), preferred_element_type=F32)
            for k in range(9):
                row = (OFFSETS - 1 - (p * 9 + k)) * CH
                total[row : row + CH] += terms[:, k * CH : (k + 1) * CH]


def rim_kernel(pos_ref, meta_ref, even_ref, odd_ref, xt_ref, total_ref, rows, keep_ref, send_ref, rims, total):
    core, own, other, odd_x = meta_ref[0], meta_ref[1], meta_ref[2], meta_ref[3]
    for i, ref in enumerate((even_ref, odd_ref)):
        at = 1 - odd_x if i == 0 else odd_x
        for r, a in enumerate(shifted(ref[0])):
            for bz in range(2):
                rims[at, r, bz] = a[:, bz]

    def clear(o, carry):
        at = pl.ds(pl.multiple_of(o * CH, CH), CH)
        total[at] = total_ref[at]
        return carry

    lax.fori_loop(0, OFFSETS + 1, clear, 0)

    for s in range(SLOTS):
        pos = pos_ref[s]
        for end, edge in ((0, 0), (1, 3)):

            @pl.when((pos >= 0) & ((pos >> 2) == edge))
            def _():
                _, by, bz = brick_of(pos)
                for r in range(3):
                    part = rims[end, r, bz, pl.ds(by * 8, 10)]
                    rows[s, :, r * CH : (r + 1) * CH] = part.reshape(PROWS, CH).astype(BF16)
                patch = jnp.concatenate([rows[s, pl.ds(q * 8, 64)] for q in range(3)], axis=1)
                blank = jnp.zeros_like(patch)
                if end == 0:
                    left, right = xt_ref[s, :, :CH], jnp.concatenate([patch, blank], axis=0)
                else:
                    left, right = xt_ref[s, :, VOX - CH :], jnp.concatenate([blank, patch], axis=0)
                terms = jnp.dot(left, right, preferred_element_type=F32)
                for k in range(9):
                    row = (OFFSETS - 1 - (18 * end + k)) * CH
                    total[row : row + CH] += terms[:, k * CH : (k + 1) * CH]

    def emit(j, carry):
        at = pl.multiple_of((core * BLOCKS + (j ^ own)) * BROWS, 8)
        keep_ref[j] = total[pl.ds(at, BROWS)]
        at = pl.multiple_of(((1 - core) * BLOCKS + (j ^ other)) * BROWS, 8)
        send_ref[j] = total[pl.ds(at, BROWS)]
        return carry

    lax.fori_loop(0, BLOCKS, emit, 0)

PATCH_SHAPE = pltpu.VMEM((SLOTS, 10, PROWS, 3 * CH), BF16)
RIM_SHAPE = pltpu.VMEM((SLOTS, PROWS, 3 * CH), BF16)
HALO = pltpu.VMEM((3, 2, NX + 2, NY + 2, 8, CH), F32)
TOTAL = pltpu.VMEM(((OFFSETS + 1) * CH, CH), F32)


def patches(slot_pos, meta, grid, sides, planes):
    return pl.pallas_call(
        patches_kernel,
        out_shape=PATCH_SHAPE,
        grid=(SLOTS,),
        in_specs=[SMEM, SMEM, HBM] + [VMEM] * 4,
        out_specs=VMEM,
        scratch_shapes=[HALO, pltpu.VMEM((NX, NY, NZ, CH), BF16), pltpu.SemaphoreType.DMA((4,))],
        compiler_params=pltpu.CompilerParams(vmem_limit_bytes=28 << 20),
        cost_estimate=pl.CostEstimate(flops=0, bytes_accessed=20 << 20, transcendentals=0),
        name="patches",
    )(slot_pos, meta, pin(grid, pltpu.HBM), *sides, *planes)


def weight_gradient(slot_pos, meta, grid, sides, xt):
    return pl.pallas_call(
        weight_kernel,
        out_shape=(PATCH_SHAPE, TOTAL),
        grid=(SLOTS,),
        in_specs=[SMEM, SMEM, HBM] + [VMEM] * 2 + [pl.BlockSpec((1, CH, VOX), lambda s: (s, 0, 0))],
        out_specs=(VMEM, VMEM),
        scratch_shapes=[HALO, pltpu.VMEM((NX, NY, NZ, CH), BF16), pltpu.SemaphoreType.DMA((4,))],
        compiler_params=pltpu.CompilerParams(vmem_limit_bytes=30 << 20),
        cost_estimate=pl.CostEstimate(flops=2 * 4096 * OFFSETS * CH * CH, bytes_accessed=20 << 20, transcendentals=0),
        name="weight_gradient",
    )(slot_pos, meta, pin(grid, pltpu.HBM), *sides, xt)


def rim_terms(slot_pos, meta, planes, xt, total):
    half = pltpu.VMEM((BLOCKS, BROWS, CH), F32)
    return pl.pallas_call(
        rim_kernel,
        out_shape=(RIM_SHAPE, half, half),
        in_specs=[SMEM, SMEM] + [VMEM] * 4,
        out_specs=(VMEM, VMEM, VMEM),
        scratch_shapes=[pltpu.VMEM((2, 3, 2, NY + 2, 8, CH), F32), TOTAL],
        compiler_params=pltpu.CompilerParams(vmem_limit_bytes=20 << 20),
        name="rim_terms",
    )(slot_pos, meta, *planes, xt, total)


def flip_kernel(w_ref, out_ref):
    for o in range(OFFSETS):
        out_ref[o * CH : (o + 1) * CH] = w_ref[OFFSETS - 1 - o].T


def flip(weights):
    return pl.pallas_call(
        flip_kernel,
        out_shape=pltpu.VMEM((OFFSETS * CH, CH), BF16),
        in_specs=[VMEM],
        out_specs=VMEM,
        compiler_params=pltpu.CompilerParams(vmem_limit_bytes=8 << 20),
        cost_estimate=pl.CostEstimate(flops=0, bytes_accessed=2 << 20, transcendentals=0),
        name="flip",
    )(weights)


def conv_kernel(first, pos_ref, occ_ref, patch_ref, rim_ref, w_ref, *rest):
    out_ref, acc = rest[-2:]
    s = first + pl.program_id(0)
    pos = pos_ref[s]

    @pl.when(pos >= 0)
    def _():
        columns = mask_columns(occ_ref)
        total = jnp.dot(patch_rows(patch_ref, s, 0), w_ref[:KROW], preferred_element_type=F32)
        for p in range(1, 3):
            total += jnp.dot(patch_rows(patch_ref, s, p), w_ref[p * KROW : (p + 1) * KROW], preferred_element_type=F32)
        acc[...] = total
        if rim_ref is not None:
            for end, edge in ((0, 0), (1, 3)):

                @pl.when((pos >> 2) == edge)
                def _():
                    rows = jnp.concatenate([rim_ref[s, pl.ds(q * 8, 64)] for q in range(3)], axis=1)
                    row, k = end * (VOX - 64), 2 * end * KROW
                    acc[row : row + 64] += jnp.dot(rows, w_ref[k : k + KROW], preferred_element_type=F32)

        lane = lax.broadcasted_iota(jnp.int32, columns.shape, 1)
        keep = jnp.sum(jnp.where(lane == s, columns, 0.0), axis=1, keepdims=True)
        out_ref[0] = jnp.where(jnp.broadcast_to(keep, (VOX, CH)) > 0.5, acc[...], 0.0).astype(BF16)

    @pl.when(pos < 0)
    def _():
        out_ref[0] = jnp.zeros((VOX, CH), BF16)


def convolve(slot_pos, occupancy, patch, rim, weights, out, first, count):
    given = [slot_pos, occupancy, pin(patch, pltpu.VMEM)] + ([] if rim is None else [pin(rim, pltpu.VMEM)]) + [pin(weights, pltpu.VMEM)]
    specs = [SMEM] + [VMEM] * (len(given) - 1)
    aliased = {}
    if out is not None:
        aliased = {len(given): 0}
        given.append(pin(out, pltpu.HBM))
        specs.append(HBM)

    def kernel(*refs):
        refs = list(refs)
        if rim is None:
            refs.insert(3, None)
        conv_kernel(first, *refs)

    return pl.pallas_call(
        kernel,
        out_shape=pltpu.HBM((SLOTS, VOX, CH), BF16),
        grid=(count,),
        in_specs=specs,
        out_specs=pl.BlockSpec((1, VOX, CH), lambda i: (first + i, 0, 0)),
        input_output_aliases=aliased,
        scratch_shapes=[pltpu.VMEM((VOX, CH), F32)],
        compiler_params=pltpu.CompilerParams(vmem_limit_bytes=12 << 20),
        cost_estimate=pl.CostEstimate(flops=count * 4 * VOX * OFFSETS * CH * CH, bytes_accessed=count << 20, transcendentals=0),
        name="convolve",
    )(*given)


def finish_kernel(mine, meta_ref, half_ref, *rest):
    out_hbm, rows, sems = rest[-3:]
    core = meta_ref[0]
    base = (core if mine else 1 - core) * BLOCKS
    order = meta_ref[1] if mine else meta_ref[2]
    scale = 1.0 / math.sqrt(float(256 * SLOTS * VOX))
    full = OFFSETS * CH // BROWS
    left = OFFSETS * CH - full * BROWS

    def copy(j, n):
        at = pl.multiple_of((base + (j ^ order)) * BROWS, 8)
        return pltpu.make_async_copy(rows.at[j, pl.ds(0, n)], out_hbm.at[pl.ds(at, n)], sems.at[j])

    def each(act):
        for j in range(BLOCKS):
            block = base + (j ^ order)

            @pl.when(block < full)
            def _():
                act(j, BROWS)

            @pl.when(block == full)
            def _():
                act(j, left)

    for j in range(BLOCKS):
        rows[j] = half_ref[j] * scale
    each(lambda j, n: copy(j, n).start())
    each(lambda j, n: copy(j, n).wait())


def finish(meta, half, out):
    given, specs = [meta, half], [SMEM, VMEM]
    if out is not None:
        given.append(pin(out, pltpu.HBM))
        specs.append(HBM)
    return pl.pallas_call(
        lambda *refs: finish_kernel(out is None, *refs),
        out_shape=pltpu.HBM((OFFSETS * CH, CH), F32),
        in_specs=specs,
        out_specs=HBM,
        input_output_aliases={} if out is None else {2: 0},
        scratch_shapes=[pltpu.VMEM((BLOCKS, BROWS, CH), F32), pltpu.SemaphoreType.DMA((BLOCKS,))],
        compiler_params=pltpu.CompilerParams(vmem_limit_bytes=8 << 20),
        cost_estimate=pl.CostEstimate(flops=0, bytes_accessed=2 << 20, transcendentals=0),
        name="finish",
    )(*given)


def make_shards(sizes):
    everyone = list(itertools.product(*[range(n) for n in sizes]))
    n_y_lo, n_core = sizes[3], sizes[4]
    narrow = n_y_lo * n_core
    wide = len(everyone) // narrow

    def number(at):
        flat = 0
        for a, n in zip(at, sizes):
            flat = flat * n + a
        return flat

    def mate(at, axis, k):
        y_hi, z, x, y_lo, core = at
        if isinstance(axis, tuple):
            axis = axis[core]
        y = y_hi * n_y_lo + y_lo
        if axis == "core":
            core ^= k
        elif axis == "x":
            x ^= k
        elif axis == "y":
            y ^= k
        else:
            z ^= k
        return (y // n_y_lo, z, x, y % n_y_lo, core)

    def swap(value, axis, k):
        return lax.ppermute(value, AXES, [(number(a), number(mate(a, axis, k))) for a in everyone])

    def exchange_wide(value, start):
        pairs = [(i * narrow + j, k * narrow + j) for a in range(start, wide - 1, 2) for i, k in ((a, a + 1), (a + 1, a)) for j in range(narrow)]
        return lax.ppermute(value, AXES, pairs)

    def exchange_narrow(value, start):
        pairs = [(i * narrow + j, i * narrow + k) for i in range(wide) for a in range(start, narrow - 1, 2) for j, k in ((a, a + 1), (a + 1, a))]
        return lax.ppermute(value, AXES, pairs)

    first, second = ("y", "x"), ("x", "y")

    def tie(*values):
        return lax.optimization_barrier(values)

    def scatter(value, axis):
        n = value.shape[0] // 4
        return [swap(value[k * n : (k + 1) * n], axis, k) for k in (2, 1, 3)]

    def add(value, parts):
        total = value[: parts[0].shape[0]]
        for part in parts:
            total = total + part
        return total

    def copies(value, axis, ks):
        return [swap(value, axis, k) for k in ks]

    def join(value, parts):
        return jnp.concatenate([value, parts[1], parts[0], parts[2]], axis=0)

    def shards(features, weights, cotangent, occupancy, slot_pos):
        slot_pos = pin(slot_pos, pltpu.HBM)
        core = lax.axis_index("core")
        x_at = lax.axis_index("x")
        y_at = lax.axis_index("y_hi") * n_y_lo + lax.axis_index("y_lo")
        yx, xy = y_at * 4 + x_at, x_at * 4 + y_at
        odd_x = x_at & 1
        meta = jnp.stack([core, jnp.where(core == 0, yx, xy), jnp.where(core == 0, xy, yx), odd_x]).astype(jnp.int32)
        xg, cg, xt, even, odd, side_even, side_odd = place(slot_pos, meta, occupancy, features, cotangent)
        side_even, side_odd, source = tie(side_even, side_odd, weights)
        side_even = exchange_narrow(side_even, 0)
        side_odd = exchange_narrow(side_odd, 1)
        side_even, side_odd, w_backward = tie(side_even, side_odd, flip(source))

        def rim(plane, last):
            ends = [jnp.where(last, v[:, NX - 1 :], v[:, :1]) for v in (side_even, side_odd)]
            first = core == 0
            return jnp.concatenate([jnp.where(first, ends[1], ends[0]), plane, jnp.where(first, ends[0], ends[1])], axis=1)

        even, odd = rim(even, odd_x == 0), rim(odd, odd_x == 1)
        even, odd, pos = tie(even, odd, slot_pos)
        even = exchange_wide(even, 0)
        odd = exchange_wide(odd, 1)
        cot_patch, total = weight_gradient(pos, meta, cg, (side_even, side_odd), xt)
        even, odd, total = tie(even, odd, total)
        cot_rim, keep, send = rim_terms(slot_pos, meta, (even, odd), xt, total)
        w_forward = weights.reshape(OFFSETS * CH, CH)
        done = {"outputs": None, "grad_input": None, "patch": None}

        def backward(at, pos):
            done["grad_input"] = convolve(pos, occupancy, cot_patch, cot_rim, w_backward, done["grad_input"], *at)
            return "grad_input"

        def forward(at, pos):
            done["outputs"] = convolve(pos, occupancy, done["patch"], None, w_forward, done["outputs"], *at)
            return "outputs"

        def gather_patches(at, pos):
            done["patch"] = patches(pos, meta, xg, (side_even, side_odd), (even, odd))
            return "patch"

        def stage(value, start, *work):
            value, pos = tie(value, slot_pos)
            parts = start(value)
            names = {call(at, pos) for call, at in work}
            held = tie(parts, *[done[n] for n in sorted(names)])
            for n, v in zip(sorted(names), held[1:]):
                done[n] = v
            return value, held[0]

        _, (got,) = stage(send, lambda v: copies(v, "core", (1,)), (backward, (0, 1)))
        total = keep + got
        total = add(*stage(total, lambda v: scatter(v, first), (backward, (1, 4))))
        total = add(*stage(total, lambda v: scatter(v, second), (backward, (5, 2))))
        total = add(*stage(total, lambda v: copies(v, "z", (2, 1, 3)), (gather_patches, None)))
        total = add(*stage(total, lambda v: copies(v, "z", (4,)), (backward, (7, 1)), (forward, (0, 1))))
        total = join(*stage(total, lambda v: copies(v, second, (2, 1, 3)), (forward, (1, 2))))
        total = join(*stage(total, lambda v: copies(v, first, (2, 1, 3)), (forward, (3, 4))))

        def finish_own(at, pos):
            done["grad_weight"] = finish(meta, total, None)
            return "grad_weight"

        total, (got,) = stage(total, lambda v: copies(v, "core", (1,)), (finish_own, None), (forward, (7, 1)))
        grad_weight = finish(meta, got, done["grad_weight"]).reshape(OFFSETS, CH, CH)
        return done["outputs"], done["grad_input"], grad_weight

    return shards


def solution(mesh):
    sizes = (2, 8, 4, 2, 2)
    fine = Mesh(mesh.devices.reshape(sizes), AXES)
    return jax.shard_map(
        make_shards(sizes),
        mesh=fine,
        in_specs=(P(AXES, None, None), P(), P(AXES, None, None), P(AXES, None), P(AXES)),
        out_specs=(P(AXES, None, None), P(AXES, None, None), P()),
        check_vma=False,
    )
```

```python
import itertools
import math

import jax
import jax.numpy as jnp
from jax import lax
from jax.experimental import pallas as pl
from jax.experimental.pallas import tpu as pltpu
from jax.sharding import Mesh, PartitionSpec as P

AXES = ("y_hi", "z", "x", "y_lo", "core")
SLOTS = 8
VOX = 512
CH = 128
NX, NY, NZ = 32, 16, 16
OFFSETS = 27
KROW = 9 * CH
BLOCKS = 16
BROWS = 112
PROWS = 80
F32 = jnp.float32
BF16 = jnp.bfloat16
VMEM = pl.BlockSpec(memory_space=pltpu.VMEM)
SMEM = pl.BlockSpec(memory_space=pltpu.SMEM)
HBM = pl.BlockSpec(memory_space=pltpu.HBM)


def pin(value, space):
    return pltpu.with_memory_space_constraint(value, space)


def brick_of(pos):
    return pos >> 2, (pos >> 1) & 1, pos & 1


def mask_columns(occ_ref):
    return jnp.where(occ_ref[...] == 1, 1.0, 0.0).astype(F32).T


def start_loads(occ_hbm, slots_hbm, occ, slots, sems):
    loads = [pltpu.make_async_copy(slots_hbm.at[s], slots.at[s], sems.at[s]) for s in range(SLOTS)]
    loads.append(pltpu.make_async_copy(occ_hbm, occ, sems.at[SLOTS]))
    for load in reversed(loads):
        load.start()
    return loads


def masked_bricks(pos_ref, loads, occ, slots, put):
    loads[SLOTS].wait()
    columns = mask_columns(occ)
    for s in range(SLOTS):
        loads[s].wait()
        pos = pos_ref[s]

        @pl.when(pos >= 0)
        def _():
            keep = jnp.broadcast_to(columns[:, s : s + 1], (VOX, CH))
            put(s, brick_of(pos), jnp.where(keep > 0.5, slots[s].astype(F32), 0.0))


def fill(pos_ref, occ_hbm, slots_hbm, cells, occ, slots, sems):
    loads = start_loads(occ_hbm, slots_hbm, occ, slots, sems)

    def clear(x, carry):
        cells[x] = jnp.zeros((NY, 2, 8, CH), F32)
        return carry

    lax.fori_loop(0, NX, clear, 0)

    def put(s, at, value):
        bx, by, bz = at
        cells[pl.ds(bx * 8, 8), pl.ds(by * 8, 8), bz] = value.reshape(8, 8, 8, CH)

    masked_bricks(pos_ref, loads, occ, slots, put)


def place_kernel(pos_ref, meta_ref, occ_hbm, feat_hbm, cot_hbm, xt, even_ref, odd_ref, side_even_ref, side_odd_ref, planes, sides, occ, slots, sems):
    core, odd_x = meta_ref[0], meta_ref[3]
    sources = (cot_hbm, feat_hbm)
    loads = [start_loads(occ_hbm, sources[t], occ.at[t], slots.at[t], sems.at[t]) for t in range(2)]
    planes[...] = jnp.zeros(planes.shape, F32)
    sides[...] = jnp.zeros(sides.shape, F32)
    for t in range(2):

        def put(s, at, value):
            bx, by, bz = at
            v = value.reshape(8, 8, 8, CH)
            sides[t, by, pl.ds(bx * 8, 8), bz] = jnp.where(by == 0, v[:, 0], v[:, 7])
            for end, edge in ((0, 0), (1, 3)):

                @pl.when(bx == edge)
                def _():
                    planes[t, end, pl.ds(by * 8, 8), bz] = v[7 * end]

            if t == 1:
                xt[s] = value.T.astype(BF16)

        masked_bricks(pos_ref, loads[t], occ.at[t], slots.at[t], put)
        even_ref[t] = planes[t, 1 - odd_x].reshape(NY, NZ, CH).astype(BF16)
        odd_ref[t] = planes[t, odd_x].reshape(NY, NZ, CH).astype(BF16)
        side_even_ref[t] = sides[t, 1 - core].reshape(NX, NZ, CH).astype(BF16)
        side_odd_ref[t] = sides[t, core].reshape(NX, NZ, CH).astype(BF16)


FILL = [
    pltpu.VMEM((NX, NY, 2, 8, CH), F32),
    pltpu.VMEM((SLOTS, VOX), jnp.int32),
    pltpu.VMEM((SLOTS, VOX, CH), BF16),
    pltpu.SemaphoreType.DMA((SLOTS + 1,)),
]


def place(slot_pos, meta, occupancy, features, cotangent):
    plane = jax.ShapeDtypeStruct((2, NY, NZ, CH), BF16)
    side = jax.ShapeDtypeStruct((2, NX, NZ, CH), BF16)
    return pl.pallas_call(
        place_kernel,
        out_shape=(pltpu.VMEM((SLOTS, CH, VOX), BF16), plane, plane, side, side),
        in_specs=[SMEM, SMEM, HBM, HBM, HBM],
        out_specs=(VMEM,) * 5,
        scratch_shapes=[
            pltpu.VMEM((2, 2, NY, 2, 8, CH), F32),
            pltpu.VMEM((2, 2, NX, 2, 8, CH), F32),
            pltpu.VMEM((2, SLOTS, VOX), jnp.int32),
            pltpu.VMEM((2, SLOTS, VOX, CH), BF16),
            pltpu.SemaphoreType.DMA((2, SLOTS + 1)),
        ],
        compiler_params=pltpu.CompilerParams(vmem_limit_bytes=20 << 20),
        name="place",
    )(slot_pos, meta, *[pin(a, pltpu.HBM) for a in (occupancy, features, cotangent)])


def shifted(v):
    n = v.shape[0]
    flat = v.astype(F32).reshape(n * NZ, CH)
    z = lax.broadcasted_iota(jnp.int32, flat.shape, 0) & (NZ - 1)
    back = jnp.where(z == 0, 0.0, pltpu.roll(flat, 1, axis=0))
    ahead = jnp.where(z == NZ - 1, 0.0, pltpu.roll(flat, n * NZ - 1, axis=0))
    return [a.reshape(n, 2, 8, CH) for a in (back, flat, ahead)]


def assemble(meta_ref, t, cells_ref, side_even_ref, side_odd_ref, halo, planes=None):
    core, odd_x = meta_ref[0], meta_ref[3]

    def body(x, carry):
        for r, a in enumerate(shifted(cells_ref[x].reshape(NY, NZ, CH))):
            for bz in range(2):
                halo[r, bz, x + 1, pl.ds(1, NY)] = a[:, bz]
        return carry

    for y, ref in (((NY + 1) * (1 - core), side_even_ref), ((NY + 1) * core, side_odd_ref)):
        for r, a in enumerate(shifted(ref[t])):
            for bz in range(2):
                halo[r, bz, pl.ds(1, NX), y] = a[:, bz]
    for i, x in enumerate(((NX + 1) * (1 - odd_x), (NX + 1) * odd_x)):
        if planes is None:
            halo[:, :, x] = jnp.zeros((3, 2, NY + 2, 8, CH), F32)
        else:
            for r, a in enumerate(shifted(planes[i][t])):
                for bz in range(2):
                    halo[r, bz, x] = a[:, bz]
    lax.fori_loop(0, NX, body, 0)


def build_patches(s, pos, halo, patch_ref):
    bx, by, bz = brick_of(pos)
    for x in range(10):
        for r in range(3):
            rows = halo[r, bz, bx * 8 + x, pl.ds(by * 8, 10)]
            patch_ref[s, x, :, r * CH : (r + 1) * CH] = rows.reshape(PROWS, CH).astype(BF16)


def patch_rows(patch_ref, s, p):
    parts = [patch_ref[s, pl.ds(p, 8), pl.ds(q * 8, 64)].reshape(VOX, 3 * CH) for q in range(3)]
    return jnp.concatenate(parts, axis=1)


def patches_kernel(pos_ref, meta_ref, occ_hbm, slots_hbm, side_even_ref, side_odd_ref, even_ref, odd_ref, patch_ref, halo, cells, occ, slots, sems):
    s = pl.program_id(0)

    @pl.when(s == 0)
    def _():
        fill(pos_ref, occ_hbm, slots_hbm, cells, occ, slots, sems)
        assemble(meta_ref, 1, cells, side_even_ref, side_odd_ref, halo, (even_ref, odd_ref))

    pos = pos_ref[s]

    @pl.when(pos >= 0)
    def _():
        build_patches(s, pos, halo, patch_ref)


def weight_kernel(pos_ref, meta_ref, occ_hbm, slots_hbm, side_even_ref, side_odd_ref, xt_ref, patch_ref, total, halo, cells, occ, slots, sems):
    s = pl.program_id(0)

    @pl.when(s == 0)
    def _():
        fill(pos_ref, occ_hbm, slots_hbm, cells, occ, slots, sems)
        assemble(meta_ref, 0, cells, side_even_ref, side_odd_ref, halo)

        def clear(o, carry):
            total[pl.ds(pl.multiple_of(o * CH, CH), CH)] = jnp.zeros((CH, CH), F32)
            return carry

        lax.fori_loop(0, OFFSETS + 1, clear, 0)

    pos = pos_ref[s]

    @pl.when(pos >= 0)
    def _():
        build_patches(s, pos, halo, patch_ref)
        for p in range(3):
            terms = jnp.dot(xt_ref[0], patch_rows(patch_ref, s, p), preferred_element_type=F32)
            for k in range(9):
                row = (OFFSETS - 1 - (p * 9 + k)) * CH
                total[row : row + CH] += terms[:, k * CH : (k + 1) * CH]


def rim_kernel(pos_ref, meta_ref, even_ref, odd_ref, xt_ref, total_ref, rows, keep_ref, send_ref, rims, total):
    core, own, other, odd_x = meta_ref[0], meta_ref[1], meta_ref[2], meta_ref[3]
    for i, ref in enumerate((even_ref, odd_ref)):
        at = 1 - odd_x if i == 0 else odd_x
        for r, a in enumerate(shifted(ref[0])):
            for bz in range(2):
                rims[at, r, bz] = a[:, bz]

    def clear(o, carry):
        at = pl.ds(pl.multiple_of(o * CH, CH), CH)
        total[at] = total_ref[at]
        return carry

    lax.fori_loop(0, OFFSETS + 1, clear, 0)

    for s in range(SLOTS):
        pos = pos_ref[s]
        for end, edge in ((0, 0), (1, 3)):

            @pl.when((pos >= 0) & ((pos >> 2) == edge))
            def _():
                _, by, bz = brick_of(pos)
                for r in range(3):
                    part = rims[end, r, bz, pl.ds(by * 8, 10)]
                    rows[s, :, r * CH : (r + 1) * CH] = part.reshape(PROWS, CH).astype(BF16)
                patch = jnp.concatenate([rows[s, pl.ds(q * 8, 64)] for q in range(3)], axis=1)
                blank = jnp.zeros_like(patch)
                if end == 0:
                    left, right = xt_ref[s, :, :CH], jnp.concatenate([patch, blank], axis=0)
                else:
                    left, right = xt_ref[s, :, VOX - CH :], jnp.concatenate([blank, patch], axis=0)
                terms = jnp.dot(left, right, preferred_element_type=F32)
                for k in range(9):
                    row = (OFFSETS - 1 - (18 * end + k)) * CH
                    total[row : row + CH] += terms[:, k * CH : (k + 1) * CH]

    def emit(j, carry):
        at = pl.multiple_of((core * BLOCKS + (j ^ own)) * BROWS, 8)
        keep_ref[j] = total[pl.ds(at, BROWS)]
        at = pl.multiple_of(((1 - core) * BLOCKS + (j ^ other)) * BROWS, 8)
        send_ref[j] = total[pl.ds(at, BROWS)]
        return carry

    lax.fori_loop(0, BLOCKS, emit, 0)

PATCH_SHAPE = pltpu.VMEM((SLOTS, 10, PROWS, 3 * CH), BF16)
RIM_SHAPE = pltpu.VMEM((SLOTS, PROWS, 3 * CH), BF16)
HALO = pltpu.VMEM((3, 2, NX + 2, NY + 2, 8, CH), F32)
TOTAL = pltpu.VMEM(((OFFSETS + 1) * CH, CH), F32)


def patches(slot_pos, meta, occupancy, slots, sides, planes):
    return pl.pallas_call(
        patches_kernel,
        out_shape=PATCH_SHAPE,
        grid=(SLOTS,),
        in_specs=[SMEM, SMEM, HBM, HBM] + [VMEM] * 4,
        out_specs=VMEM,
        scratch_shapes=[HALO] + FILL,
        compiler_params=pltpu.CompilerParams(vmem_limit_bytes=28 << 20),
        cost_estimate=pl.CostEstimate(flops=0, bytes_accessed=20 << 20, transcendentals=0),
        name="patches",
    )(slot_pos, meta, pin(occupancy, pltpu.HBM), pin(slots, pltpu.HBM), *sides, *planes)


def weight_gradient(slot_pos, meta, occupancy, slots, sides, xt):
    return pl.pallas_call(
        weight_kernel,
        out_shape=(PATCH_SHAPE, TOTAL),
        grid=(SLOTS,),
        in_specs=[SMEM, SMEM, HBM, HBM] + [VMEM] * 2 + [pl.BlockSpec((1, CH, VOX), lambda s: (s, 0, 0))],
        out_specs=(VMEM, VMEM),
        scratch_shapes=[HALO] + FILL,
        compiler_params=pltpu.CompilerParams(vmem_limit_bytes=30 << 20),
        cost_estimate=pl.CostEstimate(flops=2 * 4096 * OFFSETS * CH * CH, bytes_accessed=20 << 20, transcendentals=0),
        name="weight_gradient",
    )(slot_pos, meta, pin(occupancy, pltpu.HBM), pin(slots, pltpu.HBM), *sides, xt)


def rim_terms(slot_pos, meta, planes, xt, total):
    half = pltpu.VMEM((BLOCKS, BROWS, CH), F32)
    return pl.pallas_call(
        rim_kernel,
        out_shape=(RIM_SHAPE, half, half),
        in_specs=[SMEM, SMEM] + [VMEM] * 4,
        out_specs=(VMEM, VMEM, VMEM),
        scratch_shapes=[pltpu.VMEM((2, 3, 2, NY + 2, 8, CH), F32), TOTAL],
        compiler_params=pltpu.CompilerParams(vmem_limit_bytes=20 << 20),
        name="rim_terms",
    )(slot_pos, meta, *planes, xt, total)


def flip_kernel(w_ref, out_ref):
    for o in range(OFFSETS):
        out_ref[o * CH : (o + 1) * CH] = w_ref[OFFSETS - 1 - o].T


def flip(weights):
    return pl.pallas_call(
        flip_kernel,
        out_shape=pltpu.VMEM((OFFSETS * CH, CH), BF16),
        in_specs=[VMEM],
        out_specs=VMEM,
        compiler_params=pltpu.CompilerParams(vmem_limit_bytes=8 << 20),
        cost_estimate=pl.CostEstimate(flops=0, bytes_accessed=2 << 20, transcendentals=0),
        name="flip",
    )(weights)


def conv_kernel(first, pos_ref, occ_ref, patch_ref, rim_ref, w_ref, *rest):
    out_ref, acc = rest[-2:]
    s = first + pl.program_id(0)
    row = pos_ref[...].astype(F32)
    slot = lax.broadcasted_iota(jnp.int32, row.shape, 1)
    pos = jnp.sum(jnp.where(slot == s, row, 0.0)).astype(jnp.int32)

    @pl.when(pos >= 0)
    def _():
        columns = mask_columns(occ_ref)
        total = jnp.dot(patch_rows(patch_ref, s, 0), w_ref[:KROW], preferred_element_type=F32)
        for p in range(1, 3):
            total += jnp.dot(patch_rows(patch_ref, s, p), w_ref[p * KROW : (p + 1) * KROW], preferred_element_type=F32)
        acc[...] = total
        if rim_ref is not None:
            for end, edge in ((0, 0), (1, 3)):

                @pl.when((pos >> 2) == edge)
                def _():
                    rows = jnp.concatenate([rim_ref[s, pl.ds(q * 8, 64)] for q in range(3)], axis=1)
                    row, k = end * (VOX - 64), 2 * end * KROW
                    acc[row : row + 64] += jnp.dot(rows, w_ref[k : k + KROW], preferred_element_type=F32)

        lane = lax.broadcasted_iota(jnp.int32, columns.shape, 1)
        keep = jnp.sum(jnp.where(lane == s, columns, 0.0), axis=1, keepdims=True)
        out_ref[0] = jnp.where(jnp.broadcast_to(keep, (VOX, CH)) > 0.5, acc[...], 0.0).astype(BF16)

    @pl.when(pos < 0)
    def _():
        out_ref[0] = jnp.zeros((VOX, CH), BF16)


def convolve(slot_pos, occupancy, patch, rim, weights, out, first, count):
    given = [pin(slot_pos, pltpu.VMEM), pin(occupancy, pltpu.VMEM), pin(patch, pltpu.VMEM)] + ([] if rim is None else [pin(rim, pltpu.VMEM)]) + [pin(weights, pltpu.VMEM)]
    specs = [VMEM] * len(given)
    aliased = {}
    if out is not None:
        aliased = {len(given): 0}
        given.append(pin(out, pltpu.HBM))
        specs.append(HBM)

    def kernel(*refs):
        refs = list(refs)
        if rim is None:
            refs.insert(3, None)
        conv_kernel(first, *refs)

    return pl.pallas_call(
        kernel,
        out_shape=pltpu.HBM((SLOTS, VOX, CH), BF16),
        grid=(count,),
        in_specs=specs,
        out_specs=pl.BlockSpec((1, VOX, CH), lambda i: (first + i, 0, 0)),
        input_output_aliases=aliased,
        scratch_shapes=[pltpu.VMEM((VOX, CH), F32)],
        compiler_params=pltpu.CompilerParams(vmem_limit_bytes=12 << 20),
        cost_estimate=pl.CostEstimate(flops=count * 4 * VOX * OFFSETS * CH * CH, bytes_accessed=count << 20, transcendentals=0),
        name="convolve",
    )(*given)


def finish_kernel(mine, meta_ref, half_ref, *rest):
    out_hbm, rows, sems = rest[-3:]
    core = meta_ref[0]
    base = (core if mine else 1 - core) * BLOCKS
    order = meta_ref[1] if mine else meta_ref[2]
    scale = 1.0 / math.sqrt(float(256 * SLOTS * VOX))
    full = OFFSETS * CH // BROWS
    left = OFFSETS * CH - full * BROWS

    def copy(j, n):
        at = pl.multiple_of((base + (j ^ order)) * BROWS, 8)
        return pltpu.make_async_copy(rows.at[j, pl.ds(0, n)], out_hbm.at[pl.ds(at, n)], sems.at[j])

    def each(act):
        for j in range(BLOCKS):
            block = base + (j ^ order)

            @pl.when(block < full)
            def _():
                act(j, BROWS)

            @pl.when(block == full)
            def _():
                act(j, left)

    for j in range(BLOCKS):
        rows[j] = half_ref[j] * scale
    each(lambda j, n: copy(j, n).start())
    each(lambda j, n: copy(j, n).wait())


def finish(meta, half, out):
    given, specs = [meta, half], [SMEM, VMEM]
    if out is not None:
        given.append(pin(out, pltpu.HBM))
        specs.append(HBM)
    return pl.pallas_call(
        lambda *refs: finish_kernel(out is None, *refs),
        out_shape=pltpu.HBM((OFFSETS * CH, CH), F32),
        in_specs=specs,
        out_specs=HBM,
        input_output_aliases={} if out is None else {2: 0},
        scratch_shapes=[pltpu.VMEM((BLOCKS, BROWS, CH), F32), pltpu.SemaphoreType.DMA((BLOCKS,))],
        compiler_params=pltpu.CompilerParams(vmem_limit_bytes=8 << 20),
        cost_estimate=pl.CostEstimate(flops=0, bytes_accessed=2 << 20, transcendentals=0),
        name="finish",
    )(*given)


def make_shards(sizes):
    everyone = list(itertools.product(*[range(n) for n in sizes]))
    n_y_lo, n_core = sizes[3], sizes[4]
    narrow = n_y_lo * n_core
    wide = len(everyone) // narrow

    def number(at):
        flat = 0
        for a, n in zip(at, sizes):
            flat = flat * n + a
        return flat

    def mate(at, axis, k):
        y_hi, z, x, y_lo, core = at
        if isinstance(axis, tuple):
            axis = axis[core]
        y = y_hi * n_y_lo + y_lo
        if axis == "core":
            core ^= k
        elif axis == "x":
            x ^= k
        elif axis == "y":
            y ^= k
        else:
            z ^= k
        return (y // n_y_lo, z, x, y % n_y_lo, core)

    def swap(value, axis, k):
        return lax.ppermute(value, AXES, [(number(a), number(mate(a, axis, k))) for a in everyone])

    def exchange_wide(value, start):
        pairs = [(i * narrow + j, k * narrow + j) for a in range(start, wide - 1, 2) for i, k in ((a, a + 1), (a + 1, a)) for j in range(narrow)]
        return lax.ppermute(value, AXES, pairs)

    def exchange_narrow(value, start):
        pairs = [(i * narrow + j, i * narrow + k) for i in range(wide) for a in range(start, narrow - 1, 2) for j, k in ((a, a + 1), (a + 1, a))]
        return lax.ppermute(value, AXES, pairs)

    first, second = ("y", "x"), ("x", "y")

    def tie(*values):
        return lax.optimization_barrier(values)

    def scatter(value, axis):
        n = value.shape[0] // 4
        return [swap(value[k * n : (k + 1) * n], axis, k) for k in (2, 1, 3)]

    def add(value, parts):
        total = value[: parts[0].shape[0]]
        for part in parts:
            total = total + part
        return total

    def copies(value, axis, ks):
        return [swap(value, axis, k) for k in ks]

    def join(value, parts):
        return jnp.concatenate([value, parts[1], parts[0], parts[2]], axis=0)

    def shards(features, weights, cotangent, occupancy, slot_pos):
        slot_row = slot_pos.reshape(1, SLOTS)
        slot_pos = pin(slot_pos, pltpu.HBM)
        core = lax.axis_index("core")
        x_at = lax.axis_index("x")
        y_at = lax.axis_index("y_hi") * n_y_lo + lax.axis_index("y_lo")
        yx, xy = y_at * 4 + x_at, x_at * 4 + y_at
        odd_x = x_at & 1
        meta = jnp.stack([core, jnp.where(core == 0, yx, xy), jnp.where(core == 0, xy, yx), odd_x]).astype(jnp.int32)
        xt, even, odd, side_even, side_odd = place(slot_pos, meta, occupancy, features, cotangent)
        side_even, side_odd, source = tie(side_even, side_odd, weights)
        side_even = exchange_narrow(side_even, 0)
        side_odd = exchange_narrow(side_odd, 1)
        side_even, side_odd, w_backward = tie(side_even, side_odd, flip(source))

        def rim(plane, last):
            ends = [jnp.where(last, v[:, NX - 1 :], v[:, :1]) for v in (side_even, side_odd)]
            first = core == 0
            return jnp.concatenate([jnp.where(first, ends[1], ends[0]), plane, jnp.where(first, ends[0], ends[1])], axis=1)

        even, odd = rim(even, odd_x == 0), rim(odd, odd_x == 1)
        even, odd, pos = tie(even, odd, slot_pos)
        even = exchange_wide(even, 0)
        odd = exchange_wide(odd, 1)
        cot_patch, total = weight_gradient(pos, meta, occupancy, cotangent, (side_even, side_odd), xt)
        even, odd, total = tie(even, odd, total)
        cot_rim, keep, send = rim_terms(slot_pos, meta, (even, odd), xt, total)
        w_forward = weights.reshape(OFFSETS * CH, CH)
        done = {"outputs": None, "grad_input": None, "patch": None}

        def backward(at, row):
            done["grad_input"] = convolve(row, occupancy, cot_patch, cot_rim, w_backward, done["grad_input"], *at)
            return "grad_input"

        def forward(at, row):
            done["outputs"] = convolve(row, occupancy, done["patch"], None, w_forward, done["outputs"], *at)
            return "outputs"

        def gather_patches(at, pos):
            done["patch"] = patches(pos, meta, occupancy, features, (side_even, side_odd), (even, odd))
            return "patch"

        def stage(value, start, *work):
            value, pos, row = tie(value, slot_pos, slot_row)
            parts = start(value)
            names = {call(at, pos if at is None else row) for call, at in work}
            held = tie(parts, *[done[n] for n in sorted(names)])
            for n, v in zip(sorted(names), held[1:]):
                done[n] = v
            return value, held[0]

        _, (got,) = stage(send, lambda v: copies(v, "core", (1,)), (backward, (0, 1)))
        total = keep + got
        total = add(*stage(total, lambda v: scatter(v, first), (backward, (1, 4))))
        total = add(*stage(total, lambda v: scatter(v, second), (backward, (5, 2))))
        total = add(*stage(total, lambda v: copies(v, "z", (2, 1, 3)), (gather_patches, None)))
        total = add(*stage(total, lambda v: copies(v, "z", (4,)), (backward, (7, 1)), (forward, (0, 1))))
        total = join(*stage(total, lambda v: copies(v, second, (2, 1, 3)), (forward, (1, 2))))
        total = join(*stage(total, lambda v: copies(v, first, (2, 1, 3)), (forward, (3, 4))))

        def finish_own(at, pos):
            done["grad_weight"] = finish(meta, total, None)
            return "grad_weight"

        total, (got,) = stage(total, lambda v: copies(v, "core", (1,)), (finish_own, None), (forward, (7, 1)))
        grad_weight = finish(meta, got, done["grad_weight"]).reshape(OFFSETS, CH, CH)
        return done["outputs"], done["grad_input"], grad_weight

    return shards


def solution(mesh):
    sizes = (2, 8, 4, 2, 2)
    fine = Mesh(mesh.devices.reshape(sizes), AXES)
    return jax.shard_map(
        make_shards(sizes),
        mesh=fine,
        in_specs=(P(AXES, None, None), P(), P(AXES, None, None), P(AXES, None), P(AXES)),
        out_specs=(P(AXES, None, None), P(AXES, None, None), P()),
        check_vma=False,
    )
```

```python
import itertools
import math

import jax
import jax.numpy as jnp
from jax import lax
from jax.experimental import pallas as pl
from jax.experimental.pallas import tpu as pltpu
from jax.sharding import Mesh, PartitionSpec as P

AXES = ("y_hi", "z", "x", "y_lo", "core")
SLOTS = 8
VOX = 512
CH = 128
NX, NY, NZ = 32, 16, 16
OFFSETS = 27
KROW = 9 * CH
BLOCKS = 16
BROWS = 112
PROWS = 80
F32 = jnp.float32
BF16 = jnp.bfloat16
VMEM = pl.BlockSpec(memory_space=pltpu.VMEM)
SMEM = pl.BlockSpec(memory_space=pltpu.SMEM)
HBM = pl.BlockSpec(memory_space=pltpu.HBM)


def pin(value, space):
    return pltpu.with_memory_space_constraint(value, space)


def brick_of(pos):
    return pos >> 2, (pos >> 1) & 1, pos & 1


def mask_columns(occ_ref):
    return jnp.where(occ_ref[...] == 1, 1.0, 0.0).astype(F32).T


def start_loads(occ_hbm, slots_hbm, occ, slots, sems):
    loads = [pltpu.make_async_copy(slots_hbm.at[s], slots.at[s], sems.at[s]) for s in range(SLOTS)]
    loads.append(pltpu.make_async_copy(occ_hbm, occ, sems.at[SLOTS]))
    for load in reversed(loads):
        load.start()
    return loads


def masked_bricks(pos_ref, loads, occ, slots, put):
    loads[SLOTS].wait()
    columns = mask_columns(occ)
    for s in range(SLOTS):
        loads[s].wait()
        pos = pos_ref[s]

        @pl.when(pos >= 0)
        def _():
            keep = jnp.broadcast_to(columns[:, s : s + 1], (VOX, CH))
            put(s, brick_of(pos), jnp.where(keep > 0.5, slots[s].astype(F32), 0.0))


def fill(pos_ref, occ_hbm, slots_hbm, cells, occ, slots, sems):
    loads = start_loads(occ_hbm, slots_hbm, occ, slots, sems)

    def clear(x, carry):
        cells[x] = jnp.zeros((NY, 2, 8, CH), F32)
        return carry

    lax.fori_loop(0, NX, clear, 0)

    def put(s, at, value):
        bx, by, bz = at
        cells[pl.ds(bx * 8, 8), pl.ds(by * 8, 8), bz] = value.reshape(8, 8, 8, CH)

    masked_bricks(pos_ref, loads, occ, slots, put)


def place_kernel(pos_ref, meta_ref, occ_hbm, feat_hbm, cot_hbm, xt, even_ref, odd_ref, side_even_ref, side_odd_ref, planes, sides, occ, slots, sems):
    core, odd_x = meta_ref[0], meta_ref[3]
    sources = (cot_hbm, feat_hbm)
    loads = [start_loads(occ_hbm, sources[t], occ.at[t], slots.at[t], sems.at[t]) for t in range(2)]
    planes[...] = jnp.zeros(planes.shape, F32)
    sides[...] = jnp.zeros(sides.shape, F32)
    for t in range(2):

        def put(s, at, value):
            bx, by, bz = at
            v = value.reshape(8, 8, 8, CH)
            sides[t, by, pl.ds(bx * 8, 8), bz] = jnp.where(by == 0, v[:, 0], v[:, 7])
            for end, edge in ((0, 0), (1, 3)):

                @pl.when(bx == edge)
                def _():
                    planes[t, end, pl.ds(by * 8, 8), bz] = v[7 * end]

            if t == 1:
                xt[s] = value.T.astype(BF16)

        masked_bricks(pos_ref, loads[t], occ.at[t], slots.at[t], put)
        even_ref[t] = planes[t, 1 - odd_x].reshape(NY, NZ, CH).astype(BF16)
        odd_ref[t] = planes[t, odd_x].reshape(NY, NZ, CH).astype(BF16)
        side_even_ref[t] = sides[t, 1 - core].reshape(NX, NZ, CH).astype(BF16)
        side_odd_ref[t] = sides[t, core].reshape(NX, NZ, CH).astype(BF16)


FILL = [
    pltpu.VMEM((NX, NY, 2, 8, CH), F32),
    pltpu.VMEM((SLOTS, VOX), jnp.int32),
    pltpu.VMEM((SLOTS, VOX, CH), BF16),
    pltpu.SemaphoreType.DMA((SLOTS + 1,)),
]


def place(slot_pos, meta, occupancy, features, cotangent):
    plane = jax.ShapeDtypeStruct((2, NY, NZ, CH), BF16)
    side = jax.ShapeDtypeStruct((2, NX, NZ, CH), BF16)
    return pl.pallas_call(
        place_kernel,
        out_shape=(pltpu.VMEM((SLOTS, CH, VOX), BF16), plane, plane, side, side),
        in_specs=[SMEM, SMEM, HBM, HBM, HBM],
        out_specs=(VMEM,) * 5,
        scratch_shapes=[
            pltpu.VMEM((2, 2, NY, 2, 8, CH), F32),
            pltpu.VMEM((2, 2, NX, 2, 8, CH), F32),
            pltpu.VMEM((2, SLOTS, VOX), jnp.int32),
            pltpu.VMEM((2, SLOTS, VOX, CH), BF16),
            pltpu.SemaphoreType.DMA((2, SLOTS + 1)),
        ],
        compiler_params=pltpu.CompilerParams(vmem_limit_bytes=20 << 20),
        name="place",
    )(slot_pos, meta, *[pin(a, pltpu.HBM) for a in (occupancy, features, cotangent)])


def shifted(v):
    n = v.shape[0]
    flat = v.astype(F32).reshape(n * NZ, CH)
    z = lax.broadcasted_iota(jnp.int32, flat.shape, 0) & (NZ - 1)
    back = jnp.where(z == 0, 0.0, pltpu.roll(flat, 1, axis=0))
    ahead = jnp.where(z == NZ - 1, 0.0, pltpu.roll(flat, n * NZ - 1, axis=0))
    return [a.reshape(n, 2, 8, CH) for a in (back, flat, ahead)]


def assemble(meta_ref, t, cells_ref, side_even_ref, side_odd_ref, halo, planes):
    core, odd_x = meta_ref[0], meta_ref[3]

    def body(x, carry):
        for r, a in enumerate(shifted(cells_ref[x].reshape(NY, NZ, CH))):
            for bz in range(2):
                halo[r, bz, x + 1, pl.ds(1, NY)] = a[:, bz]
        return carry

    for y, ref in (((NY + 1) * (1 - core), side_even_ref), ((NY + 1) * core, side_odd_ref)):
        for r, a in enumerate(shifted(ref[t])):
            for bz in range(2):
                halo[r, bz, pl.ds(1, NX), y] = a[:, bz]
    for i, x in enumerate(((NX + 1) * (1 - odd_x), (NX + 1) * odd_x)):
        for r, a in enumerate(shifted(planes[i][t])):
            for bz in range(2):
                halo[r, bz, x] = a[:, bz]
    lax.fori_loop(0, NX, body, 0)


def build_patches(s, pos, halo, patch_ref):
    bx, by, bz = brick_of(pos)
    for x in range(10):
        for r in range(3):
            rows = halo[r, bz, bx * 8 + x, pl.ds(by * 8, 10)]
            patch_ref[s, x, :, r * CH : (r + 1) * CH] = rows.reshape(PROWS, CH).astype(BF16)


def patch_rows(patch_ref, s, p):
    parts = [patch_ref[s, pl.ds(p, 8), pl.ds(q * 8, 64)].reshape(VOX, 3 * CH) for q in range(3)]
    return jnp.concatenate(parts, axis=1)


def patches_kernel(pos_ref, meta_ref, occ_hbm, slots_hbm, side_even_ref, side_odd_ref, even_ref, odd_ref, patch_ref, halo, cells, occ, slots, sems):
    s = pl.program_id(0)

    @pl.when(s == 0)
    def _():
        fill(pos_ref, occ_hbm, slots_hbm, cells, occ, slots, sems)
        assemble(meta_ref, 1, cells, side_even_ref, side_odd_ref, halo, (even_ref, odd_ref))

    pos = pos_ref[s]

    @pl.when(pos >= 0)
    def _():
        build_patches(s, pos, halo, patch_ref)


def prepare_kernel(pos_ref, occ_hbm, slots_hbm, w_hbm, halo, flipped, cells, occ, slots, sems, weights, w_sem):
    load = pltpu.make_async_copy(w_hbm, weights, w_sem)
    load.start()
    fill(pos_ref, occ_hbm, slots_hbm, cells, occ, slots, sems)

    def body(x, carry):
        for r, a in enumerate(shifted(cells[x].reshape(NY, NZ, CH))):
            for bz in range(2):
                halo[r, bz, x] = a[:, bz]
        return carry

    lax.fori_loop(0, NX, body, 0)
    load.wait()
    for o in range(OFFSETS):
        flipped[o * CH : (o + 1) * CH] = weights[OFFSETS - 1 - o].T


def weight_kernel(pos_ref, meta_ref, halo, side_even_ref, side_odd_ref, xt_ref, patch_ref, total, columns):
    s = pl.program_id(0)

    @pl.when(s == 0)
    def _():
        core = meta_ref[0]
        for end, ref in ((1 - core, side_even_ref), (core, side_odd_ref)):
            for r, a in enumerate(shifted(ref[0])):
                for bz in range(2):
                    columns[end, r, bz] = a[:, bz]

        def clear(o, carry):
            total[pl.ds(pl.multiple_of(o * CH, CH), CH)] = jnp.zeros((CH, CH), F32)
            return carry

        lax.fori_loop(0, OFFSETS + 1, clear, 0)

    pos = pos_ref[s]

    @pl.when(pos >= 0)
    def _():
        bx, by, bz = brick_of(pos)
        inner = jnp.where(by == 0, 8, 7)
        for x in range(10):
            at = bx * 8 + x - 1
            for r in range(3):
                if x == 0 or x == 9:
                    valid = (at >= 0) & (at < NX)
                    near = jnp.clip(at, 0, NX - 1)
                else:
                    valid, near = None, at
                rows = halo[r, bz, near, pl.ds(by * 8, 8)]
                other = halo[r, bz, near, pl.ds(inner, 1)]
                outer = columns[by, r, bz, pl.ds(near, 1)]
                first = jnp.where(by == 0, outer, other)
                last = jnp.where(by == 0, other, outer)
                whole = jnp.concatenate([first, rows, last], axis=0)
                if valid is not None:
                    whole = jnp.where(valid, whole, 0.0)
                patch_ref[s, x, :, r * CH : (r + 1) * CH] = whole.reshape(PROWS, CH).astype(BF16)
        for p in range(3):
            terms = jnp.dot(xt_ref[0], patch_rows(patch_ref, s, p), preferred_element_type=F32)
            for k in range(9):
                row = (OFFSETS - 1 - (p * 9 + k)) * CH
                total[row : row + CH] += terms[:, k * CH : (k + 1) * CH]


def rim_kernel(pos_ref, meta_ref, even_ref, odd_ref, xt_ref, total_ref, rows, keep_ref, send_ref, rims, total):
    core, own, other, odd_x = meta_ref[0], meta_ref[1], meta_ref[2], meta_ref[3]
    for i, ref in enumerate((even_ref, odd_ref)):
        at = 1 - odd_x if i == 0 else odd_x
        for r, a in enumerate(shifted(ref[0])):
            for bz in range(2):
                rims[at, r, bz] = a[:, bz]

    def clear(o, carry):
        at = pl.ds(pl.multiple_of(o * CH, CH), CH)
        total[at] = total_ref[at]
        return carry

    lax.fori_loop(0, OFFSETS + 1, clear, 0)

    for s in range(SLOTS):
        pos = pos_ref[s]
        for end, edge in ((0, 0), (1, 3)):

            @pl.when((pos >= 0) & ((pos >> 2) == edge))
            def _():
                _, by, bz = brick_of(pos)
                for r in range(3):
                    part = rims[end, r, bz, pl.ds(by * 8, 10)]
                    rows[s, :, r * CH : (r + 1) * CH] = part.reshape(PROWS, CH).astype(BF16)
                patch = jnp.concatenate([rows[s, pl.ds(q * 8, 64)] for q in range(3)], axis=1)
                blank = jnp.zeros_like(patch)
                if end == 0:
                    left, right = xt_ref[s, :, :CH], jnp.concatenate([patch, blank], axis=0)
                else:
                    left, right = xt_ref[s, :, VOX - CH :], jnp.concatenate([blank, patch], axis=0)
                terms = jnp.dot(left, right, preferred_element_type=F32)
                for k in range(9):
                    row = (OFFSETS - 1 - (18 * end + k)) * CH
                    total[row : row + CH] += terms[:, k * CH : (k + 1) * CH]

    def emit(j, carry):
        at = pl.multiple_of((core * BLOCKS + (j ^ own)) * BROWS, 8)
        keep_ref[j] = total[pl.ds(at, BROWS)]
        at = pl.multiple_of(((1 - core) * BLOCKS + (j ^ other)) * BROWS, 8)
        send_ref[j] = total[pl.ds(at, BROWS)]
        return carry

    lax.fori_loop(0, BLOCKS, emit, 0)

PATCH_SHAPE = pltpu.VMEM((SLOTS, 10, PROWS, 3 * CH), BF16)
RIM_SHAPE = pltpu.VMEM((SLOTS, PROWS, 3 * CH), BF16)
HALO = pltpu.VMEM((3, 2, NX + 2, NY + 2, 8, CH), F32)
TOTAL = pltpu.VMEM(((OFFSETS + 1) * CH, CH), F32)


def patches(slot_pos, meta, occupancy, slots, sides, planes):
    return pl.pallas_call(
        patches_kernel,
        out_shape=PATCH_SHAPE,
        grid=(SLOTS,),
        in_specs=[SMEM, SMEM, HBM, HBM] + [VMEM] * 4,
        out_specs=VMEM,
        scratch_shapes=[HALO] + FILL,
        compiler_params=pltpu.CompilerParams(vmem_limit_bytes=28 << 20),
        cost_estimate=pl.CostEstimate(flops=0, bytes_accessed=20 << 20, transcendentals=0),
        name="patches",
    )(slot_pos, meta, pin(occupancy, pltpu.HBM), pin(slots, pltpu.HBM), *sides, *planes)


PREPARED = pltpu.VMEM((3, 2, NX, NY, 8, CH), F32)


def prepare(slot_pos, occupancy, slots, weights):
    return pl.pallas_call(
        prepare_kernel,
        out_shape=(PREPARED, pltpu.VMEM((OFFSETS * CH, CH), BF16)),
        in_specs=[SMEM, HBM, HBM, HBM],
        out_specs=(VMEM, VMEM),
        scratch_shapes=FILL + [pltpu.VMEM((OFFSETS, CH, CH), BF16), pltpu.SemaphoreType.DMA],
        compiler_params=pltpu.CompilerParams(vmem_limit_bytes=26 << 20),
        cost_estimate=pl.CostEstimate(flops=0, bytes_accessed=8 << 20, transcendentals=0),
        name="prepare",
    )(slot_pos, *[pin(a, pltpu.HBM) for a in (occupancy, slots, weights)])


def weight_gradient(slot_pos, meta, prepared, sides, xt):
    return pl.pallas_call(
        weight_kernel,
        out_shape=(PATCH_SHAPE, TOTAL),
        grid=(SLOTS,),
        in_specs=[SMEM, SMEM] + [VMEM] * 3 + [pl.BlockSpec((1, CH, VOX), lambda s: (s, 0, 0))],
        out_specs=(VMEM, VMEM),
        scratch_shapes=[pltpu.VMEM((2, 3, 2, NX, 8, CH), F32)],
        compiler_params=pltpu.CompilerParams(vmem_limit_bytes=30 << 20),
        cost_estimate=pl.CostEstimate(flops=2 * 4096 * OFFSETS * CH * CH, bytes_accessed=20 << 20, transcendentals=0),
        name="weight_gradient",
    )(slot_pos, meta, pin(prepared, pltpu.VMEM), *sides, xt)


def rim_terms(slot_pos, meta, planes, xt, total):
    half = pltpu.VMEM((BLOCKS, BROWS, CH), F32)
    return pl.pallas_call(
        rim_kernel,
        out_shape=(RIM_SHAPE, half, half),
        in_specs=[SMEM, SMEM] + [VMEM] * 4,
        out_specs=(VMEM, VMEM, VMEM),
        scratch_shapes=[pltpu.VMEM((2, 3, 2, NY + 2, 8, CH), F32), TOTAL],
        compiler_params=pltpu.CompilerParams(vmem_limit_bytes=20 << 20),
        name="rim_terms",
    )(slot_pos, meta, *planes, xt, total)


def conv_kernel(first, pos_ref, occ_ref, patch_ref, rim_ref, w_ref, *rest):
    out_ref, acc = rest[-2:]
    s = first + pl.program_id(0)
    row = pos_ref[...].astype(F32)
    slot = lax.broadcasted_iota(jnp.int32, row.shape, 1)
    pos = jnp.sum(jnp.where(slot == s, row, 0.0)).astype(jnp.int32)

    @pl.when(pos >= 0)
    def _():
        columns = mask_columns(occ_ref)
        total = jnp.dot(patch_rows(patch_ref, s, 0), w_ref[:KROW], preferred_element_type=F32)
        for p in range(1, 3):
            total += jnp.dot(patch_rows(patch_ref, s, p), w_ref[p * KROW : (p + 1) * KROW], preferred_element_type=F32)
        acc[...] = total
        if rim_ref is not None:
            for end, edge in ((0, 0), (1, 3)):

                @pl.when((pos >> 2) == edge)
                def _():
                    rows = jnp.concatenate([rim_ref[s, pl.ds(q * 8, 64)] for q in range(3)], axis=1)
                    row, k = end * (VOX - 64), 2 * end * KROW
                    acc[row : row + 64] += jnp.dot(rows, w_ref[k : k + KROW], preferred_element_type=F32)

        lane = lax.broadcasted_iota(jnp.int32, columns.shape, 1)
        keep = jnp.sum(jnp.where(lane == s, columns, 0.0), axis=1, keepdims=True)
        out_ref[0] = jnp.where(jnp.broadcast_to(keep, (VOX, CH)) > 0.5, acc[...], 0.0).astype(BF16)

    @pl.when(pos < 0)
    def _():
        out_ref[0] = jnp.zeros((VOX, CH), BF16)


def convolve(slot_pos, occupancy, patch, rim, weights, out, first, count):
    given = [pin(slot_pos, pltpu.VMEM), pin(occupancy, pltpu.VMEM), pin(patch, pltpu.VMEM)] + ([] if rim is None else [pin(rim, pltpu.VMEM)]) + [pin(weights, pltpu.VMEM)]
    specs = [VMEM] * len(given)
    aliased = {}
    if out is not None:
        aliased = {len(given): 0}
        given.append(pin(out, pltpu.HBM))
        specs.append(HBM)

    def kernel(*refs):
        refs = list(refs)
        if rim is None:
            refs.insert(3, None)
        conv_kernel(first, *refs)

    return pl.pallas_call(
        kernel,
        out_shape=pltpu.HBM((SLOTS, VOX, CH), BF16),
        grid=(count,),
        in_specs=specs,
        out_specs=pl.BlockSpec((1, VOX, CH), lambda i: (first + i, 0, 0)),
        input_output_aliases=aliased,
        scratch_shapes=[pltpu.VMEM((VOX, CH), F32)],
        compiler_params=pltpu.CompilerParams(vmem_limit_bytes=12 << 20),
        cost_estimate=pl.CostEstimate(flops=count * 4 * VOX * OFFSETS * CH * CH, bytes_accessed=count << 20, transcendentals=0),
        name="convolve",
    )(*given)


def finish_kernel(mine, meta_ref, half_ref, *rest):
    out_hbm, rows, sems = rest[-3:]
    core = meta_ref[0]
    base = (core if mine else 1 - core) * BLOCKS
    order = meta_ref[1] if mine else meta_ref[2]
    scale = 1.0 / math.sqrt(float(256 * SLOTS * VOX))
    full = OFFSETS * CH // BROWS
    left = OFFSETS * CH - full * BROWS

    def copy(j, n):
        at = pl.multiple_of((base + (j ^ order)) * BROWS, 8)
        return pltpu.make_async_copy(rows.at[j, pl.ds(0, n)], out_hbm.at[pl.ds(at, n)], sems.at[j])

    def each(act):
        for j in range(BLOCKS):
            block = base + (j ^ order)

            @pl.when(block < full)
            def _():
                act(j, BROWS)

            @pl.when(block == full)
            def _():
                act(j, left)

    for j in range(BLOCKS):
        rows[j] = half_ref[j] * scale
    each(lambda j, n: copy(j, n).start())
    each(lambda j, n: copy(j, n).wait())


def finish(meta, half, out):
    given, specs = [meta, half], [SMEM, VMEM]
    if out is not None:
        given.append(pin(out, pltpu.HBM))
        specs.append(HBM)
    return pl.pallas_call(
        lambda *refs: finish_kernel(out is None, *refs),
        out_shape=pltpu.HBM((OFFSETS * CH, CH), F32),
        in_specs=specs,
        out_specs=HBM,
        input_output_aliases={} if out is None else {2: 0},
        scratch_shapes=[pltpu.VMEM((BLOCKS, BROWS, CH), F32), pltpu.SemaphoreType.DMA((BLOCKS,))],
        compiler_params=pltpu.CompilerParams(vmem_limit_bytes=8 << 20),
        cost_estimate=pl.CostEstimate(flops=0, bytes_accessed=2 << 20, transcendentals=0),
        name="finish",
    )(*given)


def make_shards(sizes):
    everyone = list(itertools.product(*[range(n) for n in sizes]))
    n_y_lo, n_core = sizes[3], sizes[4]
    narrow = n_y_lo * n_core
    wide = len(everyone) // narrow

    def number(at):
        flat = 0
        for a, n in zip(at, sizes):
            flat = flat * n + a
        return flat

    def mate(at, axis, k):
        y_hi, z, x, y_lo, core = at
        if isinstance(axis, tuple):
            axis = axis[core]
        y = y_hi * n_y_lo + y_lo
        if axis == "core":
            core ^= k
        elif axis == "x":
            x ^= k
        elif axis == "y":
            y ^= k
        else:
            z ^= k
        return (y // n_y_lo, z, x, y % n_y_lo, core)

    def swap(value, axis, k):
        return lax.ppermute(value, AXES, [(number(a), number(mate(a, axis, k))) for a in everyone])

    def exchange_wide(value, start):
        pairs = [(i * narrow + j, k * narrow + j) for a in range(start, wide - 1, 2) for i, k in ((a, a + 1), (a + 1, a)) for j in range(narrow)]
        return lax.ppermute(value, AXES, pairs)

    def exchange_narrow(value, start):
        pairs = [(i * narrow + j, i * narrow + k) for i in range(wide) for a in range(start, narrow - 1, 2) for j, k in ((a, a + 1), (a + 1, a))]
        return lax.ppermute(value, AXES, pairs)

    first, second = ("y", "x"), ("x", "y")

    def tie(*values):
        return lax.optimization_barrier(values)

    def scatter(value, axis):
        n = value.shape[0] // 4
        return [swap(value[k * n : (k + 1) * n], axis, k) for k in (2, 1, 3)]

    def add(value, parts):
        total = value[: parts[0].shape[0]]
        for part in parts:
            total = total + part
        return total

    def copies(value, axis, ks):
        return [swap(value, axis, k) for k in ks]

    def join(value, parts):
        return jnp.concatenate([value, parts[1], parts[0], parts[2]], axis=0)

    def shards(features, weights, cotangent, occupancy, slot_pos):
        slot_row = slot_pos.reshape(1, SLOTS)
        slot_pos = pin(slot_pos, pltpu.HBM)
        core = lax.axis_index("core")
        x_at = lax.axis_index("x")
        y_at = lax.axis_index("y_hi") * n_y_lo + lax.axis_index("y_lo")
        yx, xy = y_at * 4 + x_at, x_at * 4 + y_at
        odd_x = x_at & 1
        meta = jnp.stack([core, jnp.where(core == 0, yx, xy), jnp.where(core == 0, xy, yx), odd_x]).astype(jnp.int32)
        xt, even, odd, side_even, side_odd = place(slot_pos, meta, occupancy, features, cotangent)
        side_even, side_odd, pos = tie(side_even, side_odd, slot_pos)
        side_even = exchange_narrow(side_even, 0)
        side_odd = exchange_narrow(side_odd, 1)
        prepared, w_backward = prepare(pos, occupancy, cotangent, weights)
        side_even, side_odd, w_backward = tie(side_even, side_odd, w_backward)

        def rim(plane, last):
            ends = [jnp.where(last, v[:, NX - 1 :], v[:, :1]) for v in (side_even, side_odd)]
            first = core == 0
            return jnp.concatenate([jnp.where(first, ends[1], ends[0]), plane, jnp.where(first, ends[0], ends[1])], axis=1)

        even, odd = rim(even, odd_x == 0), rim(odd, odd_x == 1)
        even, odd, pos = tie(even, odd, slot_pos)
        even = exchange_wide(even, 0)
        odd = exchange_wide(odd, 1)
        cot_patch, total = weight_gradient(pos, meta, prepared, (side_even, side_odd), xt)
        even, odd, total = tie(even, odd, total)
        cot_rim, keep, send = rim_terms(slot_pos, meta, (even, odd), xt, total)
        w_forward = weights.reshape(OFFSETS * CH, CH)
        done = {"outputs": None, "grad_input": None, "patch": None}

        def backward(at, row):
            done["grad_input"] = convolve(row, occupancy, cot_patch, cot_rim, w_backward, done["grad_input"], *at)
            return "grad_input"

        def forward(at, row):
            done["outputs"] = convolve(row, occupancy, done["patch"], None, w_forward, done["outputs"], *at)
            return "outputs"

        def gather_patches(at, pos):
            done["patch"] = patches(pos, meta, occupancy, features, (side_even, side_odd), (even, odd))
            return "patch"

        def stage(value, start, *work):
            value, pos, row = tie(value, slot_pos, slot_row)
            parts = start(value)
            names = {call(at, pos if at is None else row) for call, at in work}
            held = tie(parts, *[done[n] for n in sorted(names)])
            for n, v in zip(sorted(names), held[1:]):
                done[n] = v
            return value, held[0]

        _, (got,) = stage(send, lambda v: copies(v, "core", (1,)), (backward, (0, 1)))
        total = keep + got
        total = add(*stage(total, lambda v: scatter(v, first), (backward, (1, 3))))
        total = add(*stage(total, lambda v: scatter(v, second), (backward, (4, 3))))
        total = add(*stage(total, lambda v: copies(v, "z", (2, 1, 3)), (gather_patches, None)))
        total = add(*stage(total, lambda v: copies(v, "z", (4,)), (backward, (7, 1)), (forward, (0, 2))))
        total = join(*stage(total, lambda v: copies(v, second, (2, 1, 3)), (forward, (2, 2))))
        total = join(*stage(total, lambda v: copies(v, first, (2, 1, 3)), (forward, (4, 4))))

        def finish_own(at, pos):
            done["grad_weight"] = finish(meta, total, None)
            return "grad_weight"

        total, (got,) = stage(total, lambda v: copies(v, "core", (1,)), (finish_own, None))
        grad_weight = finish(meta, got, done["grad_weight"]).reshape(OFFSETS, CH, CH)
        return done["outputs"], done["grad_input"], grad_weight

    return shards


def solution(mesh):
    sizes = (2, 8, 4, 2, 2)
    fine = Mesh(mesh.devices.reshape(sizes), AXES)
    return jax.shard_map(
        make_shards(sizes),
        mesh=fine,
        in_specs=(P(AXES, None, None), P(), P(AXES, None, None), P(AXES, None), P(AXES)),
        out_specs=(P(AXES, None, None), P(AXES, None, None), P()),
        check_vma=False,
    )
```

```python
import itertools
import math

import jax
import jax.numpy as jnp
from jax import lax
from jax.experimental import pallas as pl
from jax.experimental.pallas import tpu as pltpu
from jax.sharding import Mesh, PartitionSpec as P

AXES = ("y_hi", "z", "x", "y_lo", "core")
SLOTS = 8
VOX = 512
CH = 128
NX, NY, NZ = 32, 16, 16
OFFSETS = 27
KROW = 9 * CH
BLOCKS = 16
BROWS = 112
PROWS = 80
F32 = jnp.float32
BF16 = jnp.bfloat16
VMEM = pl.BlockSpec(memory_space=pltpu.VMEM)
SMEM = pl.BlockSpec(memory_space=pltpu.SMEM)
HBM = pl.BlockSpec(memory_space=pltpu.HBM)


def pin(value, space):
    return pltpu.with_memory_space_constraint(value, space)


def brick_of(pos):
    return pos >> 2, (pos >> 1) & 1, pos & 1


def mask_columns(occ_ref):
    return jnp.where(occ_ref[...] == 1, 1.0, 0.0).astype(F32).T


def start_loads(occ_hbm, slots_hbm, occ, slots, sems):
    loads = [pltpu.make_async_copy(slots_hbm.at[s], slots.at[s], sems.at[s]) for s in range(SLOTS)]
    loads.append(pltpu.make_async_copy(occ_hbm, occ, sems.at[SLOTS]))
    for load in reversed(loads):
        load.start()
    return loads


def masked_bricks(pos_ref, loads, occ, slots, put):
    loads[SLOTS].wait()
    columns = mask_columns(occ)
    for s in range(SLOTS):
        loads[s].wait()
        pos = pos_ref[s]

        @pl.when(pos >= 0)
        def _():
            keep = jnp.broadcast_to(columns[:, s : s + 1], (VOX, CH))
            put(s, brick_of(pos), jnp.where(keep > 0.5, slots[s].astype(F32), 0.0))


def fill(pos_ref, occ_hbm, slots_hbm, cells, occ, slots, sems):
    loads = start_loads(occ_hbm, slots_hbm, occ, slots, sems)

    def clear(x, carry):
        cells[x] = jnp.zeros((NY, 2, 8, CH), F32)
        return carry

    lax.fori_loop(0, NX, clear, 0)

    def put(s, at, value):
        bx, by, bz = at
        cells[pl.ds(bx * 8, 8), pl.ds(by * 8, 8), bz] = value.reshape(8, 8, 8, CH)

    masked_bricks(pos_ref, loads, occ, slots, put)


def place_kernel(pos_ref, meta_ref, occ_hbm, feat_hbm, cot_hbm, xt, even_ref, odd_ref, side_even_ref, side_odd_ref, planes, sides, occ, slots, sems):
    core, odd_x = meta_ref[0], meta_ref[3]
    sources = (cot_hbm, feat_hbm)
    loads = [start_loads(occ_hbm, sources[t], occ.at[t], slots.at[t], sems.at[t]) for t in range(2)]
    planes[...] = jnp.zeros(planes.shape, F32)
    sides[...] = jnp.zeros(sides.shape, F32)
    for t in range(2):

        def put(s, at, value):
            bx, by, bz = at
            v = value.reshape(8, 8, 8, CH)
            sides[t, by, pl.ds(bx * 8, 8), bz] = jnp.where(by == 0, v[:, 0], v[:, 7])
            for end, edge in ((0, 0), (1, 3)):

                @pl.when(bx == edge)
                def _():
                    planes[t, end, pl.ds(by * 8, 8), bz] = v[7 * end]

            if t == 1:
                xt[s] = value.T.astype(BF16)

        masked_bricks(pos_ref, loads[t], occ.at[t], slots.at[t], put)
        even_ref[t] = planes[t, 1 - odd_x].reshape(NY, NZ, CH).astype(BF16)
        odd_ref[t] = planes[t, odd_x].reshape(NY, NZ, CH).astype(BF16)
        side_even_ref[t] = sides[t, 1 - core].reshape(NX, NZ, CH).astype(BF16)
        side_odd_ref[t] = sides[t, core].reshape(NX, NZ, CH).astype(BF16)


FILL = [
    pltpu.VMEM((NX, NY, 2, 8, CH), F32),
    pltpu.VMEM((SLOTS, VOX), jnp.int32),
    pltpu.VMEM((SLOTS, VOX, CH), BF16),
    pltpu.SemaphoreType.DMA((SLOTS + 1,)),
]


def place(slot_pos, meta, occupancy, features, cotangent):
    plane = jax.ShapeDtypeStruct((2, NY, NZ, CH), BF16)
    side = jax.ShapeDtypeStruct((2, NX, NZ, CH), BF16)
    return pl.pallas_call(
        place_kernel,
        out_shape=(pltpu.VMEM((SLOTS, CH, VOX), BF16), plane, plane, side, side),
        in_specs=[SMEM, SMEM, HBM, HBM, HBM],
        out_specs=(VMEM,) * 5,
        scratch_shapes=[
            pltpu.VMEM((2, 2, NY, 2, 8, CH), F32),
            pltpu.VMEM((2, 2, NX, 2, 8, CH), F32),
            pltpu.VMEM((2, SLOTS, VOX), jnp.int32),
            pltpu.VMEM((2, SLOTS, VOX, CH), BF16),
            pltpu.SemaphoreType.DMA((2, SLOTS + 1)),
        ],
        compiler_params=pltpu.CompilerParams(vmem_limit_bytes=10 << 20),
        name="place",
    )(slot_pos, meta, *[pin(a, pltpu.HBM) for a in (occupancy, features, cotangent)])


def shifted(v):
    n = v.shape[0]
    flat = v.astype(F32).reshape(n * NZ, CH)
    z = lax.broadcasted_iota(jnp.int32, flat.shape, 0) & (NZ - 1)
    back = jnp.where(z == 0, 0.0, pltpu.roll(flat, 1, axis=0))
    ahead = jnp.where(z == NZ - 1, 0.0, pltpu.roll(flat, n * NZ - 1, axis=0))
    return [a.reshape(n, 2, 8, CH) for a in (back, flat, ahead)]


def assemble(meta_ref, t, cells_ref, side_even_ref, side_odd_ref, halo, planes):
    core, odd_x = meta_ref[0], meta_ref[3]

    def body(x, carry):
        for r, a in enumerate(shifted(cells_ref[x].reshape(NY, NZ, CH))):
            for bz in range(2):
                halo[r, bz, x + 1, pl.ds(1, NY)] = a[:, bz]
        return carry

    for y, ref in (((NY + 1) * (1 - core), side_even_ref), ((NY + 1) * core, side_odd_ref)):
        for r, a in enumerate(shifted(ref[t])):
            for bz in range(2):
                halo[r, bz, pl.ds(1, NX), y] = a[:, bz]
    for i, x in enumerate(((NX + 1) * (1 - odd_x), (NX + 1) * odd_x)):
        for r, a in enumerate(shifted(planes[i][t])):
            for bz in range(2):
                halo[r, bz, x] = a[:, bz]
    lax.fori_loop(0, NX, body, 0)


def build_patches(s, pos, halo, patch_ref):
    bx, by, bz = brick_of(pos)
    for x in range(10):
        for r in range(3):
            rows = halo[r, bz, bx * 8 + x, pl.ds(by * 8, 10)]
            patch_ref[s, x, :, r * CH : (r + 1) * CH] = rows.reshape(PROWS, CH).astype(BF16)


def patch_rows(patch_ref, s, p):
    parts = [patch_ref[s, pl.ds(p, 8), pl.ds(q * 8, 64)].reshape(VOX, 3 * CH) for q in range(3)]
    return jnp.concatenate(parts, axis=1)


def patches_kernel(pos_ref, meta_ref, occ_hbm, slots_hbm, side_even_ref, side_odd_ref, even_ref, odd_ref, patch_ref, halo, cells, occ, slots, sems):
    s = pl.program_id(0)

    @pl.when(s == 0)
    def _():
        fill(pos_ref, occ_hbm, slots_hbm, cells, occ, slots, sems)
        assemble(meta_ref, 1, cells, side_even_ref, side_odd_ref, halo, (even_ref, odd_ref))

    pos = pos_ref[s]

    @pl.when(pos >= 0)
    def _():
        build_patches(s, pos, halo, patch_ref)


def prepare_kernel(pos_ref, occ_hbm, slots_hbm, w_hbm, halo, flipped, cells, occ, slots, sems, weights, w_sem):
    load = pltpu.make_async_copy(w_hbm, weights, w_sem)
    load.start()
    fill(pos_ref, occ_hbm, slots_hbm, cells, occ, slots, sems)

    def body(x, carry):
        for r, a in enumerate(shifted(cells[x].reshape(NY, NZ, CH))):
            for bz in range(2):
                halo[r, bz, x] = a[:, bz]
        return carry

    lax.fori_loop(0, NX, body, 0)
    load.wait()
    for o in range(OFFSETS):
        flipped[o * CH : (o + 1) * CH] = weights[OFFSETS - 1 - o].T


def weight_kernel(pos_ref, meta_ref, halo, side_even_ref, side_odd_ref, xt_ref, patch_ref, total, columns):
    s = pl.program_id(0)

    @pl.when(s == 0)
    def _():
        core = meta_ref[0]
        for end, ref in ((1 - core, side_even_ref), (core, side_odd_ref)):
            for r, a in enumerate(shifted(ref[0])):
                for bz in range(2):
                    columns[end, r, bz] = a[:, bz]

        def clear(o, carry):
            total[pl.ds(pl.multiple_of(o * CH, CH), CH)] = jnp.zeros((CH, CH), F32)
            return carry

        lax.fori_loop(0, OFFSETS + 1, clear, 0)

    pos = pos_ref[s]

    @pl.when(pos >= 0)
    def _():
        bx, by, bz = brick_of(pos)
        inner = jnp.where(by == 0, 8, 7)
        for x in range(10):
            at = bx * 8 + x - 1
            for r in range(3):
                if x == 0 or x == 9:
                    valid = (at >= 0) & (at < NX)
                    near = jnp.clip(at, 0, NX - 1)
                else:
                    valid, near = None, at
                rows = halo[r, bz, near, pl.ds(by * 8, 8)]
                other = halo[r, bz, near, pl.ds(inner, 1)]
                outer = columns[by, r, bz, pl.ds(near, 1)]
                first = jnp.where(by == 0, outer, other)
                last = jnp.where(by == 0, other, outer)
                whole = jnp.concatenate([first, rows, last], axis=0)
                if valid is not None:
                    whole = jnp.where(valid, whole, 0.0)
                patch_ref[s, x, :, r * CH : (r + 1) * CH] = whole.reshape(PROWS, CH).astype(BF16)
        for p in range(3):
            terms = jnp.dot(xt_ref[0], patch_rows(patch_ref, s, p), preferred_element_type=F32)
            for k in range(9):
                row = (OFFSETS - 1 - (p * 9 + k)) * CH
                total[row : row + CH] += terms[:, k * CH : (k + 1) * CH]


def rim_kernel(pos_ref, meta_ref, even_ref, odd_ref, xt_ref, total_ref, rows, keep_ref, send_ref, rims, total):
    core, own, other, odd_x = meta_ref[0], meta_ref[1], meta_ref[2], meta_ref[3]
    for i, ref in enumerate((even_ref, odd_ref)):
        at = 1 - odd_x if i == 0 else odd_x
        for r, a in enumerate(shifted(ref[0])):
            for bz in range(2):
                rims[at, r, bz] = a[:, bz]

    def clear(o, carry):
        at = pl.ds(pl.multiple_of(o * CH, CH), CH)
        total[at] = total_ref[at]
        return carry

    lax.fori_loop(0, OFFSETS + 1, clear, 0)

    for s in range(SLOTS):
        pos = pos_ref[s]
        for end, edge in ((0, 0), (1, 3)):

            @pl.when((pos >= 0) & ((pos >> 2) == edge))
            def _():
                _, by, bz = brick_of(pos)
                for r in range(3):
                    part = rims[end, r, bz, pl.ds(by * 8, 10)]
                    rows[s, :, r * CH : (r + 1) * CH] = part.reshape(PROWS, CH).astype(BF16)
                patch = jnp.concatenate([rows[s, pl.ds(q * 8, 64)] for q in range(3)], axis=1)
                blank = jnp.zeros_like(patch)
                if end == 0:
                    left, right = xt_ref[s, :, :CH], jnp.concatenate([patch, blank], axis=0)
                else:
                    left, right = xt_ref[s, :, VOX - CH :], jnp.concatenate([blank, patch], axis=0)
                terms = jnp.dot(left, right, preferred_element_type=F32)
                for k in range(9):
                    row = (OFFSETS - 1 - (18 * end + k)) * CH
                    total[row : row + CH] += terms[:, k * CH : (k + 1) * CH]

    def emit(j, carry):
        at = pl.multiple_of((core * BLOCKS + (j ^ own)) * BROWS, 8)
        keep_ref[j] = total[pl.ds(at, BROWS)]
        at = pl.multiple_of(((1 - core) * BLOCKS + (j ^ other)) * BROWS, 8)
        send_ref[j] = total[pl.ds(at, BROWS)]
        return carry

    lax.fori_loop(0, BLOCKS, emit, 0)

PATCH_SHAPE = pltpu.VMEM((SLOTS, 10, PROWS, 3 * CH), BF16)
RIM_SHAPE = pltpu.VMEM((SLOTS, PROWS, 3 * CH), BF16)
HALO = pltpu.VMEM((3, 2, NX + 2, NY + 2, 8, CH), F32)
TOTAL = pltpu.VMEM(((OFFSETS + 1) * CH, CH), F32)


def patches(slot_pos, meta, occupancy, slots, sides, planes):
    return pl.pallas_call(
        patches_kernel,
        out_shape=PATCH_SHAPE,
        grid=(SLOTS,),
        in_specs=[SMEM, SMEM, HBM, HBM] + [VMEM] * 4,
        out_specs=VMEM,
        scratch_shapes=[HALO] + FILL,
        compiler_params=pltpu.CompilerParams(vmem_limit_bytes=24 << 20),
        cost_estimate=pl.CostEstimate(flops=0, bytes_accessed=20 << 20, transcendentals=0),
        name="patches",
    )(slot_pos, meta, pin(occupancy, pltpu.HBM), pin(slots, pltpu.HBM), *sides, *planes)


PREPARED = pltpu.VMEM((3, 2, NX, NY, 8, CH), F32)


def prepare(slot_pos, occupancy, slots, weights):
    return pl.pallas_call(
        prepare_kernel,
        out_shape=(PREPARED, pltpu.VMEM((OFFSETS * CH, CH), BF16)),
        in_specs=[SMEM, HBM, HBM, HBM],
        out_specs=(VMEM, VMEM),
        scratch_shapes=FILL + [pltpu.VMEM((OFFSETS, CH, CH), BF16), pltpu.SemaphoreType.DMA],
        compiler_params=pltpu.CompilerParams(vmem_limit_bytes=24 << 20),
        cost_estimate=pl.CostEstimate(flops=0, bytes_accessed=8 << 20, transcendentals=0),
        name="prepare",
    )(slot_pos, *[pin(a, pltpu.HBM) for a in (occupancy, slots, weights)])


def weight_gradient(slot_pos, meta, prepared, sides, xt):
    return pl.pallas_call(
        weight_kernel,
        out_shape=(PATCH_SHAPE, TOTAL),
        grid=(SLOTS,),
        in_specs=[SMEM, SMEM] + [VMEM] * 3 + [pl.BlockSpec((1, CH, VOX), lambda s: (s, 0, 0))],
        out_specs=(VMEM, VMEM),
        scratch_shapes=[pltpu.VMEM((2, 3, 2, NX, 8, CH), F32)],
        compiler_params=pltpu.CompilerParams(vmem_limit_bytes=10 << 20),
        cost_estimate=pl.CostEstimate(flops=2 * 4096 * OFFSETS * CH * CH, bytes_accessed=20 << 20, transcendentals=0),
        name="weight_gradient",
    )(slot_pos, meta, pin(prepared, pltpu.VMEM), *sides, xt)


def rim_terms(slot_pos, meta, planes, xt, total):
    half = pltpu.VMEM((BLOCKS, BROWS, CH), F32)
    return pl.pallas_call(
        rim_kernel,
        out_shape=(RIM_SHAPE, half, half),
        in_specs=[SMEM, SMEM] + [VMEM] * 4,
        out_specs=(VMEM, VMEM, VMEM),
        scratch_shapes=[pltpu.VMEM((2, 3, 2, NY + 2, 8, CH), F32), TOTAL],
        compiler_params=pltpu.CompilerParams(vmem_limit_bytes=8 << 20),
        name="rim_terms",
    )(slot_pos, meta, *planes, xt, total)


def conv_kernel(first, pos_ref, occ_ref, patch_ref, rim_ref, w_ref, *rest):
    out_ref, acc = rest[-2:]
    s = first + pl.program_id(0)
    row = pos_ref[...].astype(F32)
    slot = lax.broadcasted_iota(jnp.int32, row.shape, 1)
    pos = jnp.sum(jnp.where(slot == s, row, 0.0)).astype(jnp.int32)

    @pl.when(pos >= 0)
    def _():
        columns = mask_columns(occ_ref)
        total = jnp.dot(patch_rows(patch_ref, s, 0), w_ref[:KROW], preferred_element_type=F32)
        for p in range(1, 3):
            total += jnp.dot(patch_rows(patch_ref, s, p), w_ref[p * KROW : (p + 1) * KROW], preferred_element_type=F32)
        acc[...] = total
        if rim_ref is not None:
            for end, edge in ((0, 0), (1, 3)):

                @pl.when((pos >> 2) == edge)
                def _():
                    rows = jnp.concatenate([rim_ref[s, pl.ds(q * 8, 64)] for q in range(3)], axis=1)
                    row, k = end * (VOX - 64), 2 * end * KROW
                    acc[row : row + 64] += jnp.dot(rows, w_ref[k : k + KROW], preferred_element_type=F32)

        lane = lax.broadcasted_iota(jnp.int32, columns.shape, 1)
        keep = jnp.sum(jnp.where(lane == s, columns, 0.0), axis=1, keepdims=True)
        out_ref[0] = jnp.where(jnp.broadcast_to(keep, (VOX, CH)) > 0.5, acc[...], 0.0).astype(BF16)

    @pl.when(pos < 0)
    def _():
        out_ref[0] = jnp.zeros((VOX, CH), BF16)


def convolve(slot_pos, occupancy, patch, rim, weights, out, first, count):
    given = [pin(slot_pos, pltpu.VMEM), pin(occupancy, pltpu.VMEM), pin(patch, pltpu.VMEM)] + ([] if rim is None else [pin(rim, pltpu.VMEM)]) + [pin(weights, pltpu.VMEM)]
    specs = [VMEM] * len(given)
    aliased = {}
    if out is not None:
        aliased = {len(given): 0}
        given.append(pin(out, pltpu.HBM))
        specs.append(HBM)

    def kernel(*refs):
        refs = list(refs)
        if rim is None:
            refs.insert(3, None)
        conv_kernel(first, *refs)

    return pl.pallas_call(
        kernel,
        out_shape=pltpu.HBM((SLOTS, VOX, CH), BF16),
        grid=(count,),
        in_specs=specs,
        out_specs=pl.BlockSpec((1, VOX, CH), lambda i: (first + i, 0, 0)),
        input_output_aliases=aliased,
        scratch_shapes=[pltpu.VMEM((VOX, CH), F32)],
        compiler_params=pltpu.CompilerParams(vmem_limit_bytes=6 << 20),
        cost_estimate=pl.CostEstimate(flops=count * 4 * VOX * OFFSETS * CH * CH, bytes_accessed=count << 20, transcendentals=0),
        name="convolve",
    )(*given)


def finish_kernel(mine, meta_ref, half_ref, *rest):
    out_hbm, rows, sems = rest[-3:]
    core = meta_ref[0]
    base = (core if mine else 1 - core) * BLOCKS
    order = meta_ref[1] if mine else meta_ref[2]
    scale = 1.0 / math.sqrt(float(256 * SLOTS * VOX))
    full = OFFSETS * CH // BROWS
    left = OFFSETS * CH - full * BROWS

    def copy(j, n):
        at = pl.multiple_of((base + (j ^ order)) * BROWS, 8)
        return pltpu.make_async_copy(rows.at[j, pl.ds(0, n)], out_hbm.at[pl.ds(at, n)], sems.at[j])

    def each(act):
        for j in range(BLOCKS):
            block = base + (j ^ order)

            @pl.when(block < full)
            def _():
                act(j, BROWS)

            @pl.when(block == full)
            def _():
                act(j, left)

    for j in range(BLOCKS):
        rows[j] = half_ref[j] * scale
    each(lambda j, n: copy(j, n).start())
    each(lambda j, n: copy(j, n).wait())


def finish(meta, half, out):
    given, specs = [meta, half], [SMEM, VMEM]
    if out is not None:
        given.append(pin(out, pltpu.HBM))
        specs.append(HBM)
    return pl.pallas_call(
        lambda *refs: finish_kernel(out is None, *refs),
        out_shape=pltpu.HBM((OFFSETS * CH, CH), F32),
        in_specs=specs,
        out_specs=HBM,
        input_output_aliases={} if out is None else {2: 0},
        scratch_shapes=[pltpu.VMEM((BLOCKS, BROWS, CH), F32), pltpu.SemaphoreType.DMA((BLOCKS,))],
        compiler_params=pltpu.CompilerParams(vmem_limit_bytes=8 << 20),
        cost_estimate=pl.CostEstimate(flops=0, bytes_accessed=2 << 20, transcendentals=0),
        name="finish",
    )(*given)


def make_shards(sizes):
    everyone = list(itertools.product(*[range(n) for n in sizes]))
    n_y_lo, n_core = sizes[3], sizes[4]
    narrow = n_y_lo * n_core
    wide = len(everyone) // narrow

    def number(at):
        flat = 0
        for a, n in zip(at, sizes):
            flat = flat * n + a
        return flat

    def mate(at, axis, k):
        y_hi, z, x, y_lo, core = at
        if isinstance(axis, tuple):
            axis = axis[core]
        y = y_hi * n_y_lo + y_lo
        if axis == "core":
            core ^= k
        elif axis == "x":
            x ^= k
        elif axis == "y":
            y ^= k
        else:
            z ^= k
        return (y // n_y_lo, z, x, y % n_y_lo, core)

    def swap(value, axis, k):
        return lax.ppermute(value, AXES, [(number(a), number(mate(a, axis, k))) for a in everyone])

    def exchange_wide(value, start):
        pairs = [(i * narrow + j, k * narrow + j) for a in range(start, wide - 1, 2) for i, k in ((a, a + 1), (a + 1, a)) for j in range(narrow)]
        return lax.ppermute(value, AXES, pairs)

    def exchange_narrow(value, start):
        pairs = [(i * narrow + j, i * narrow + k) for i in range(wide) for a in range(start, narrow - 1, 2) for j, k in ((a, a + 1), (a + 1, a))]
        return lax.ppermute(value, AXES, pairs)

    first, second = ("y", "x"), ("x", "y")

    def tie(*values):
        return lax.optimization_barrier(values)

    def scatter(value, axis):
        n = value.shape[0] // 4
        return [swap(value[k * n : (k + 1) * n], axis, k) for k in (2, 1, 3)]

    def add(value, parts):
        total = value[: parts[0].shape[0]]
        for part in parts:
            total = total + part
        return total

    def copies(value, axis, ks):
        return [swap(value, axis, k) for k in ks]

    def join(value, parts):
        return jnp.concatenate([value, parts[1], parts[0], parts[2]], axis=0)

    def shards(features, weights, cotangent, occupancy, slot_pos):
        slot_row = slot_pos.reshape(1, SLOTS)
        slot_pos = pin(slot_pos, pltpu.HBM)
        core = lax.axis_index("core")
        x_at = lax.axis_index("x")
        y_at = lax.axis_index("y_hi") * n_y_lo + lax.axis_index("y_lo")
        yx, xy = y_at * 4 + x_at, x_at * 4 + y_at
        odd_x = x_at & 1
        meta = jnp.stack([core, jnp.where(core == 0, yx, xy), jnp.where(core == 0, xy, yx), odd_x]).astype(jnp.int32)
        xt, even, odd, side_even, side_odd = place(slot_pos, meta, occupancy, features, cotangent)
        side_even, side_odd, pos = tie(side_even, side_odd, slot_pos)
        side_even = exchange_narrow(side_even, 0)
        side_odd = exchange_narrow(side_odd, 1)
        prepared, w_backward = prepare(pos, occupancy, cotangent, weights)
        side_even, side_odd, w_backward = tie(side_even, side_odd, w_backward)

        def rim(plane, last):
            ends = [jnp.where(last, v[:, NX - 1 :], v[:, :1]) for v in (side_even, side_odd)]
            first = core == 0
            return jnp.concatenate([jnp.where(first, ends[1], ends[0]), plane, jnp.where(first, ends[0], ends[1])], axis=1)

        even, odd = rim(even, odd_x == 0), rim(odd, odd_x == 1)
        even, odd, pos = tie(even, odd, slot_pos)
        even = exchange_wide(even, 0)
        odd = exchange_wide(odd, 1)
        cot_patch, total = weight_gradient(pos, meta, prepared, (side_even, side_odd), xt)
        even, odd, total = tie(even, odd, total)
        cot_rim, keep, send = rim_terms(slot_pos, meta, (even, odd), xt, total)
        w_forward = weights.reshape(OFFSETS * CH, CH)
        done = {"outputs": None, "grad_input": None, "patch": None}

        def backward(at, row):
            done["grad_input"] = convolve(row, occupancy, cot_patch, cot_rim, w_backward, done["grad_input"], *at)
            return "grad_input"

        def forward(at, row):
            done["outputs"] = convolve(row, occupancy, done["patch"], None, w_forward, done["outputs"], *at)
            return "outputs"

        def gather_patches(at, pos):
            done["patch"] = patches(pos, meta, occupancy, features, (side_even, side_odd), (even, odd))
            return "patch"

        def stage(value, start, *work):
            value, pos, row = tie(value, slot_pos, slot_row)
            parts = start(value)
            names = {call(at, pos if at is None else row) for call, at in work}
            held = tie(parts, *[done[n] for n in sorted(names)])
            for n, v in zip(sorted(names), held[1:]):
                done[n] = v
            return value, held[0]

        _, (got,) = stage(send, lambda v: copies(v, "core", (1,)), (backward, (0, 1)))
        total = keep + got
        total = add(*stage(total, lambda v: scatter(v, first), (backward, (1, 3))))
        total = add(*stage(total, lambda v: scatter(v, second), (backward, (4, 3))))
        total = add(*stage(total, lambda v: copies(v, "z", (2, 1, 3)), (gather_patches, None)))
        total = add(*stage(total, lambda v: copies(v, "z", (4,)), (backward, (7, 1)), (forward, (0, 2))))
        total = join(*stage(total, lambda v: copies(v, second, (2, 1, 3)), (forward, (2, 2))))
        total = join(*stage(total, lambda v: copies(v, first, (2, 1, 3)), (forward, (4, 4))))

        def finish_own(at, pos):
            done["grad_weight"] = finish(meta, total, None)
            return "grad_weight"

        total, (got,) = stage(total, lambda v: copies(v, "core", (1,)), (finish_own, None))
        grad_weight = finish(meta, got, done["grad_weight"]).reshape(OFFSETS, CH, CH)
        return done["outputs"], done["grad_input"], grad_weight

    return shards


def solution(mesh):
    sizes = (2, 8, 4, 2, 2)
    fine = Mesh(mesh.devices.reshape(sizes), AXES)
    return jax.shard_map(
        make_shards(sizes),
        mesh=fine,
        in_specs=(P(AXES, None, None), P(), P(AXES, None, None), P(AXES, None), P(AXES)),
        out_specs=(P(AXES, None, None), P(AXES, None, None), P()),
        check_vma=False,
    )
```
